1024 devices in a mesh: wave: 16 (over z, core), lev: 64 (over x, y).
Axes of the slice: x: 8, y: 8, z: 8, core: 2. Of those that a mesh axis runs over, the one named last changes fastest.
Arguments:
- grid_values: bfloat16 [256, 480, 1024], P('lev', 'wave'), may hold values from -6 to 6
- legendre: bfloat16 [160, 480, 384], P('wave'), as said below
- gauss_weights: float32 [480], replicated, may hold values from 0.5 to 1.5
- modes_in: bfloat16 [128, 128], replicated, may hold values from -0.5 to 0.5
- modes_out: bfloat16 [128, 128], replicated, may hold values from -0.5 to 0.5
- stiffness: float32 [128], replicated, may hold values from 0.1 to 10
- slot_pair: int32 [160], replicated, may hold values from 0 to 159, each once
- lat_order: int32 [480], replicated, may hold values from 0 to 479, each once
- field_slots: int32 [256], replicated, may hold values from 0 to 255, each once
Outputs:
- product: bfloat16 [256, 480, 1024], P('lev', 'wave')
The draws below stay inside these ranges and needn't reach their ends.
Inputs may be any that keep to these rules, and one draw needn't show every extreme that they name: legendre is zero in every column c > 320. `slot_pair`: a permutation. `lat_order`: a permutation. `field_slots`: a permutation.
All inputs are finite; a program needn't handle non-finite values.
Results may differ from the reference program's by a relative error of at most 0.0085.
Values may be sent and summed in bfloat16 or wider, within the bound.
A program may use at most 32 MiB of HBM per device.

```python
import math
import jax
import jax.numpy as jnp
from jax import lax

NLAT = 480
NLON = 1024
NM = 320
LEVELS = 128
PAIRS = 160
KP = 384
FL = 256


def draw_legendre(key, part):
    array_shape = (PAIRS, NLAT, KP)
    values = jnp.clip(jax.random.normal(key, array_shape, jnp.float32), -6.0, 6.0) / math.sqrt(NLAT)
    valid_column = jnp.arange(KP) <= NM
    return jnp.where(valid_column[None, None, :], values, 0.0).astype(jnp.bfloat16)


def shard_levels(own_key, shape, pieces, low, top_value):
    def one(axis_at, parts):
        heights = jax.random.uniform(jax.random.fold_in(jax.random.fold_in(own_key, 6), axis_at), (parts,), jnp.float32, low / len(pieces), top_value / len(pieces))
        return jnp.repeat(jnp.exp(heights), shape[axis_at] // parts).reshape((-1,) + (1,) * (len(shape) - axis_at - 1))

    factor_of = one(*pieces[0])
    for cut in pieces[1:]:
        factor_of = factor_of * one(*cut)
    return factor_of


def centred(own_key, shape, spread, reach, cuts=(), held_as=jnp.bfloat16):
    gain = shard_levels(own_key, shape, cuts, -0.22, 0.18) if cuts else 1.0
    drawn = jax.random.normal(own_key, shape, jnp.float32) * spread * gain
    return jnp.minimum(jnp.maximum(drawn, -reach), reach).astype(held_as)


def setup_inputs(seed: int = 0) -> dict:
    seeds = jax.random.split(jax.random.key(seed), 10)
    return {
        "grid_values": centred(seeds[0], (FL, NLAT, NLON), 1.0, 6.0, ((0, 64), (1, 16))),
        "legendre": draw_legendre(jax.random.fold_in(seeds[9], 71), 0),
        "gauss_weights": jnp.clip(jax.random.uniform(seeds[2], (NLAT,), jnp.float32, 0.5, 1.5), 0.5, 1.5),
        "modes_in": centred(seeds[3], (LEVELS, LEVELS), LEVELS ** -0.5, 0.5),
        "modes_out": centred(seeds[4], (LEVELS, LEVELS), LEVELS ** -0.5, 0.5),
        "stiffness": jnp.clip(jnp.exp(jax.random.uniform(seeds[5], (LEVELS,), jnp.float32, math.log(0.1), math.log(10.0))), 0.1, 10.0),
        "slot_pair": jax.random.permutation(seeds[6], PAIRS).astype(jnp.int32),
        "lat_order": jax.random.permutation(seeds[7], NLAT).astype(jnp.int32),
        "field_slots": jax.random.permutation(seeds[8], FL).astype(jnp.int32),
    }


def fourier_table(wavenumbers, longitudes):
    lon_index = jnp.arange(longitudes, dtype=jnp.int32)
    phase_steps = lon_index[:, None] * wavenumbers[None, :] % longitudes
    angles = phase_steps.astype(jnp.float32) * (2.0 * jnp.pi / longitudes)
    scaling = 1.0 / jnp.sqrt(jnp.float32(longitudes))
    entries = jnp.stack([jnp.cos(angles), -jnp.sin(angles)], axis=2) * scaling
    return entries.astype(jnp.bfloat16).reshape(longitudes, 2 * wavenumbers.shape[0])

def reference(grid_values, legendre, gauss_weights, modes_in, modes_out, stiffness, slot_pair, lat_order, field_slots):
    row_count, lat_count, lon_count = grid_values.shape
    column_count = legendre.shape[2]
    wave_table = fourier_table(jnp.arange(NM, dtype=jnp.int32), lon_count)
    row_weight = gauss_weights[lat_order]
    fourier = jnp.dot(grid_values.reshape(row_count * lat_count, lon_count), wave_table, preferred_element_type=jnp.float32)
    fourier = (fourier.reshape(row_count, lat_count, NM, 2) * row_weight[None, :, None, None]).astype(jnp.bfloat16)
    fourier_true = jnp.zeros_like(fourier).at[:, lat_order].set(fourier)
    column = jnp.arange(column_count, dtype=jnp.int32)

    def forward_slot(inputs):
        basis_slot, pair_index = inputs
        first_half = column < NM - pair_index
        basis_wide = basis_slot.astype(jnp.float32)
        lower_wave = jnp.take(fourier_true, pair_index, axis=2).astype(jnp.float32)
        upper_wave = jnp.take(fourier_true, NM - 1 - pair_index, axis=2).astype(jnp.float32)
        lower_part = jnp.einsum('rji,jc->ric', lower_wave, basis_wide)
        upper_part = jnp.einsum('rji,jc->ric', upper_wave, basis_wide)
        return jnp.where(first_half, lower_part, upper_part).astype(jnp.bfloat16)
    spectral = lax.map(forward_slot, (legendre, slot_pair))
    spectral_rows = jnp.moveaxis(spectral, 0, 1)
    ordered = jnp.zeros_like(spectral_rows).at[field_slots].set(spectral_rows)
    pair_column = slot_pair[:, None]
    degree = jnp.where(column[None, :] < NM - pair_column, pair_column + column[None, :], column[None, :] - 1).astype(jnp.float32)
    growth = degree * (degree + 1.0) / (NM * NM)
    factor = 1.0 / (1.0 + growth[None, :, None, :] * stiffness[:, None, None, None])
    fields_count = row_count // LEVELS
    stacked = ordered.reshape(fields_count, LEVELS, slot_pair.shape[0], 2, column_count).astype(jnp.float32)
    projected = jnp.einsum('ml,flkic->fmkic', modes_in.astype(jnp.float32), stacked)
    modal_values = (projected * factor[None]).astype(jnp.bfloat16)
    restored = jnp.einsum('lm,fmkic->flkic', modes_out.astype(jnp.float32), modal_values.astype(jnp.float32)).astype(jnp.bfloat16)
    implicit = restored.reshape(row_count, slot_pair.shape[0], 2, column_count)[field_slots]

    def backward_slot(inputs):
        basis_slot, pair_index, coefficients = inputs
        first_half = column < NM - pair_index
        basis_wide = basis_slot.astype(jnp.float32)
        coeff_wide = coefficients.astype(jnp.float32)
        lower_part = jnp.einsum('ric,jc->rji', jnp.where(first_half, coeff_wide, 0.0), basis_wide)
        upper_part = jnp.einsum('ric,jc->rji', jnp.where(first_half, 0.0, coeff_wide), basis_wide)
        return (lower_part.astype(jnp.bfloat16), upper_part.astype(jnp.bfloat16))
    lower_all, upper_all = lax.map(backward_slot, (legendre, slot_pair, jnp.moveaxis(implicit, 1, 0)))
    back_true = jnp.zeros((row_count, lat_count, NM, 2), jnp.bfloat16)
    back_true = back_true.at[:, :, slot_pair].set(jnp.moveaxis(lower_all, 0, 2))
    back_true = back_true.at[:, :, NM - 1 - slot_pair].set(jnp.moveaxis(upper_all, 0, 2))
    fourier_back = back_true[:, lat_order]
    field_values = lax.dot_general(fourier_back.reshape(row_count * lat_count, 2 * NM), wave_table, (((1,), (1,)), ((), ())), preferred_element_type=jnp.float32)
    product = field_values.reshape(row_count, lat_count, lon_count) * grid_values.astype(jnp.float32)
    return product.astype(jnp.bfloat16)
```

```python
import functools

import jax
import jax.numpy as jnp
import numpy as np
from jax import lax
from jax.experimental import pallas as pl
from jax.experimental.pallas import tpu as pltpu
from jax.sharding import PartitionSpec as P

NM = 320
LEVELS = 128
W = 16
LV = 64
ROWS = 4
JL = 30
JP = 32
SLOTS = 10
LAT = 480
COLS = 384
NB = 60
NLON = 1024
F32 = jnp.float32
BF16 = jnp.bfloat16
MESH = pl.DeviceIdType.MESH
HBM = pl.BlockSpec(memory_space=pltpu.HBM)
VMEM = pl.BlockSpec(memory_space=pltpu.VMEM)
SMEM = pl.BlockSpec(memory_space=pltpu.SMEM)
DMA = pltpu.SemaphoreType.DMA


def fourier_rows():
    steps = (np.arange(NM)[:, None] * np.arange(NLON)[None, :]) % NLON
    angles = steps.astype(np.float32) * np.float32(2.0 * np.pi / NLON)
    entries = np.stack([np.cos(angles), -np.sin(angles)], axis=1) / np.float32(32.0)
    return entries.reshape(2 * NM, NLON).astype(jnp.bfloat16)


def iota(shape, axis):
    return lax.broadcasted_iota(jnp.int32, shape, axis)


def one_hot(condition):
    return jnp.where(condition, 1.0, 0.0).astype(F32).astype(BF16)


def dot(a, b):
    return jnp.dot(a, b, preferred_element_type=F32)


def dot_nt(a, b):
    return lax.dot_general(a, b, (((1,), (1,)), ((), ())), preferred_element_type=F32)


def signal_axis(axis, size):
    me = lax.axis_index(axis)
    barrier = pltpu.get_barrier_semaphore()

    def send(i, carry):
        pl.semaphore_signal(
            barrier, inc=1, device_id={axis: lax.rem(me + i, size)}, device_id_type=MESH
        )
        return carry

    lax.fori_loop(1, size, send, 0)


def wait_axis(size):
    pl.semaphore_wait(pltpu.get_barrier_semaphore(), size - 1)


def lat_selector(lat_ref):
    lat = lat_ref[...]
    j = iota((LAT, W * JP), 0)
    jp = iota((LAT, W * JP), 1)
    local = jp & (JP - 1)
    spread = one_hot((j == (jp >> 5) * JL + local) & (local < JL))
    high = jnp.broadcast_to((lat >> 5).astype(F32), (8, LAT)).astype(BF16)
    low = jnp.broadcast_to((lat & 31).astype(F32), (8, LAT)).astype(BF16)
    there = dot(high, spread)[0:1] * 32.0 + dot(low, spread)[0:1]
    there = jnp.where((iota((1, W * JP), 1) & (JP - 1)) < JL, there, -1.0)
    return one_hot(iota((LAT, W * JP), 0).astype(F32) == there)


def rows_to_lanes(pieces):
    return [
        jnp.concatenate([piece[:, JP * b : JP * b + JP] for piece in pieces], axis=1)
        for b in range(4)
    ]


def load_grid(grid_ref, spread):
    spread[...] = jnp.zeros_like(spread)
    for jl in range(JL):
        rows = grid_ref[jl].astype(F32)
        for b in range(8):
            spread[b, pl.ds(jl, ROWS, stride=JP), :] = rows[:, 128 * b : 128 * b + 128]


def joined(ref):
    return jnp.concatenate([ref[b] for b in range(ref.shape[0])], axis=1)


def exchange_wave(send_buf, recv_buf, send_sem, recv_sem):
    w = lax.axis_index("wave")

    def send(i, carry):
        to = lax.rem(w + i, W)
        pltpu.make_async_remote_copy(
            src_ref=send_buf.at[to],
            dst_ref=recv_buf.at[w],
            send_sem=send_sem,
            recv_sem=recv_sem,
            device_id={"wave": to},
            device_id_type=MESH,
        ).start()
        return carry

    lax.fori_loop(1, W, send, 0)
    recv_buf[w] = send_buf[w]


def wait_bytes(ref, count, sem):
    part = ref.at[pl.ds(0, count)]
    pltpu.make_async_copy(part, part, sem).wait()


def kernel_a(
    lat_s, gauss_s, lat_ref, pair_ref, grid_hbm, table_hbm, out_ref,
    grid_v, table_v, spread, send_buf, recv_buf, mixed, copy_sem, send_sem, recv_sem,
):
    w = lax.axis_index("wave")
    signal_axis("wave", W)
    get_grid = pltpu.make_async_copy(grid_hbm, grid_v, copy_sem.at[0])
    get_table = pltpu.make_async_copy(table_hbm, table_v, copy_sem.at[1])
    get_grid.start()
    get_table.start()

    lane = iota((1, 128), 1)

    def add_weight(jl, weight):
        value = gauss_s[lat_s[w * JL + jl]]
        return jnp.where((lane & (JP - 1)) == jl, value, weight)

    weight = lax.fori_loop(0, JL, add_weight, jnp.zeros((1, 128), F32))

    pair = jnp.broadcast_to(pair_ref[...].astype(F32), (128, 160)).astype(BF16)
    repeat = one_hot((iota((640, 160), 0) >> 2) == iota((640, 160), 1))
    pair_col = dot_nt(repeat, pair)
    i = iota((640, 128), 0)
    wave = jnp.where((i & 2) == 0, pair_col, (NM - 1.0) - pair_col)
    target = 2.0 * wave + (i & 1).astype(F32)
    to_slots = jnp.concatenate(
        [one_hot(target == (iota((640, 128), 1) + 128 * b).astype(F32)) for b in range(5)],
        axis=1,
    )

    get_grid.wait()
    load_grid(grid_v, spread)
    values = joined(spread).astype(BF16)
    get_table.wait()
    fourier = (dot_nt(table_v[...], values) * weight).astype(BF16)
    slotted = dot(to_slots, fourier)
    for d in range(W):
        send_buf[d] = slotted[40 * d : 40 * d + 40].astype(BF16)

    wait_axis(W)
    exchange_wave(send_buf, recv_buf, send_sem, recv_sem)
    selector = lat_selector(lat_ref)
    wait_bytes(recv_buf, W - 1, recv_sem)
    for g in range(4):
        pieces = rows_to_lanes([recv_buf[4 * g + s].astype(F32) for s in range(4)])
        for r in range(ROWS):
            mixed[g, pl.ds(r, 40, stride=ROWS), :] = pieces[r]
    out_ref[...] = dot_nt(joined(mixed).astype(BF16), selector).astype(BF16)
    wait_bytes(send_buf, W - 1, send_sem)


def exchange_lev(send_buf, recv_buf, send_sem, recv_sem, limit):
    me = lax.axis_index("lev")

    def send(i, carry):
        to = lax.rem(me + i, LV)

        @pl.when(to < limit)
        def _():
            pltpu.make_async_remote_copy(
                src_ref=send_buf.at[to],
                dst_ref=recv_buf.at[me],
                send_sem=send_sem,
                recv_sem=recv_sem,
                device_id={"lev": to},
                device_id_type=MESH,
            ).start()

        return carry

    lax.fori_loop(1, LV, send, 0)


def kernel_b(
    pair_s, slots_ref, stiff_ref, in_ref, modes_in_ref, modes_out_ref, basis_hbm, out_ref,
    basis, out_buf, in_buf, back_buf, home_buf, rows_f, copy_sem, send_sem, recv_sem,
):
    w = lax.axis_index("wave")
    me = lax.axis_index("lev")
    works = me < NB
    signal_axis("lev", LV)
    gets = [
        pltpu.make_async_copy(basis_hbm.at[k], basis.at[k], copy_sem.at[k]) for k in range(SLOTS)
    ]
    for get in gets:
        get.start()

    slots = slots_ref[...]
    picks = [
        one_hot((iota((LEVELS, 256), 0) + LEVELS * f) == slots) for f in range(2)
    ]
    modes_in = jnp.concatenate([dot(modes_in_ref[...], pick) for pick in picks], axis=0)
    modes_in = modes_in.astype(BF16)
    modes_out_t = jnp.transpose(modes_out_ref[...].astype(F32)).astype(BF16)
    modes_out = jnp.concatenate([dot(modes_out_t, pick) for pick in picks], axis=0)
    modes_out = jnp.transpose(modes_out).astype(BF16)
    stiffness = jnp.transpose(jnp.broadcast_to(stiff_ref[...], (128, 128)))
    own = lax.min(me, NB - 1)
    own_pair = pair_s[w * SLOTS + own // 6]
    column = iota((1, 128), 1) + (own % 3) * 128
    degree = jnp.where(column < NM - own_pair, own_pair + column, column - 1).astype(F32)
    growth = degree * (degree + 1.0) / (NM * NM)
    factor = 1.0 / (1.0 + growth * stiffness)

    all_columns = iota((8, COLS), 1)
    for k in range(SLOTS):
        gets[k].wait()
        both = dot(in_ref[16 * k : 16 * k + 16], basis[k])
        first = all_columns < NM - pair_s[w * SLOTS + k]
        picked = jnp.where(first, both[0:8], both[8:16])
        for q in range(2):
            for c in range(3):
                out_buf[6 * k + 3 * q + c] = picked[
                    4 * q : 4 * q + 4, 128 * c : 128 * c + 128
                ].astype(BF16)

    wait_axis(LV)
    exchange_lev(out_buf, in_buf, send_sem.at[0], recv_sem.at[0], NB)

    @pl.when(works)
    def _():
        in_buf[me] = out_buf[me]
        wait_bytes(in_buf, LV - 1, recv_sem.at[0])
        for s in range(LV):
            rows_f[4 * s : 4 * s + 4] = in_buf[s].astype(F32)
        modal = dot(modes_in, rows_f[...].astype(BF16))
        modal = jnp.concatenate([modal[:128] * factor, modal[128:] * factor], axis=0)
        rows_f[...] = dot(modes_out, modal.astype(BF16))
        for s in range(LV):
            back_buf[s] = rows_f[4 * s : 4 * s + 4].astype(BF16)
        exchange_lev(back_buf, home_buf, send_sem.at[1], recv_sem.at[1], LV)
        home_buf[me] = back_buf[me]
        wait_bytes(home_buf, NB - 1, recv_sem.at[1])
        wait_bytes(out_buf, NB - 1, send_sem.at[0])
        wait_bytes(back_buf, LV - 1, send_sem.at[1])

    @pl.when(jnp.logical_not(works))
    def _():
        wait_bytes(home_buf, NB, recv_sem.at[1])
        wait_bytes(out_buf, NB, send_sem.at[0])

    for k in range(SLOTS):
        for q in range(2):
            for c in range(3):
                out_ref[8 * k + 4 * q : 8 * k + 4 * q + 4, 128 * c : 128 * c + 128] = home_buf[
                    6 * k + 3 * q + c
                ].astype(F32)


def kernel_c(
    pair_s, lat_ref, pair_ref, in_ref, basis_hbm, grid_hbm, table_hbm, out_ref,
    basis, grid_v, table_v, spread, back, mixed, send_buf, recv_buf, slotted, copy_sem, send_sem,
    recv_sem,
):
    w = lax.axis_index("wave")
    signal_axis("wave", W)
    gets = [
        pltpu.make_async_copy(basis_hbm.at[k], basis.at[k], copy_sem.at[k]) for k in range(SLOTS)
    ]
    for get in gets:
        get.start()
    get_grid = pltpu.make_async_copy(grid_hbm, grid_v, copy_sem.at[SLOTS])
    get_table = pltpu.make_async_copy(table_hbm, table_v, copy_sem.at[SLOTS + 1])
    get_grid.start()
    get_table.start()

    all_columns = iota((8, COLS), 1)
    for k in range(SLOTS):
        values = in_ref[8 * k : 8 * k + 8]
        first = all_columns < NM - pair_s[w * SLOTS + k]
        both = jnp.concatenate(
            [jnp.where(first, values, 0.0), jnp.where(first, 0.0, values)], axis=0
        ).astype(BF16)
        gets[k].wait()
        back[16 * k : 16 * k + 16] = dot_nt(both, basis[k]).astype(BF16)
    there = dot(back[...], lat_selector(lat_ref))
    for g in range(4):
        mixed[g] = there[:, 128 * g : 128 * g + 128]
    for g in range(4):
        pieces = rows_to_lanes(
            [mixed[g, pl.ds(r, 40, stride=ROWS), :] for r in range(ROWS)]
        )
        for s in range(4):
            send_buf[4 * g + s] = pieces[s].astype(BF16)
    wait_axis(W)
    exchange_wave(send_buf, recv_buf, send_sem, recv_sem)

    pair = jnp.broadcast_to(pair_ref[...].astype(F32), (8, 160)).astype(BF16)
    repeat = one_hot(iota((160, 640), 0) == (iota((160, 640), 1) >> 2))
    pair_row = dot(pair, repeat)[0:1]
    i = iota((1, 640), 1)
    wave = jnp.where((i & 2) == 0, pair_row, (NM - 1.0) - pair_row)
    target = 2.0 * wave + (i & 1).astype(F32)
    from_slots = one_hot(iota((640, 640), 0).astype(F32) == target)
    get_grid.wait()
    load_grid(grid_v, spread)
    get_table.wait()

    wait_bytes(recv_buf, W - 1, recv_sem)
    for d in range(W):
        slotted[40 * d : 40 * d + 40] = recv_buf[d].astype(F32)
    natural = dot(from_slots, slotted[...].astype(BF16))
    fields = dot(jnp.transpose(natural).astype(BF16), table_v[...])
    for b in range(8):
        spread[b] = spread[b] * fields[:, 128 * b : 128 * b + 128]
    for jl in range(JL):
        for b in range(8):
            rows = spread[b, pl.ds(jl, ROWS, stride=JP), :]
            out_ref[jl, :, 128 * b : 128 * b + 128] = rows.astype(BF16)
    wait_bytes(send_buf, W - 1, send_sem)


def params(collective_id):
    return pltpu.CompilerParams(
        collective_id=collective_id, has_side_effects=True, vmem_limit_bytes=60 << 20
    )


def local(
    grid_values,
    legendre,
    gauss_weights,
    modes_in,
    modes_out,
    stiffness,
    slot_pair,
    lat_order,
    field_slots,
):
    table = jnp.asarray(fourier_rows())
    grid = jnp.transpose(grid_values, (1, 0, 2))
    lat_row = lat_order.reshape(1, LAT)
    pair_row = slot_pair.reshape(1, 160)
    grouped = pl.pallas_call(
        kernel_a,
        out_shape=jax.ShapeDtypeStruct((160, LAT), BF16),
        in_specs=[SMEM, SMEM, VMEM, VMEM, HBM, HBM],
        out_specs=VMEM,
        scratch_shapes=[
            pltpu.VMEM((JL, ROWS, NLON), BF16),
            pltpu.VMEM((640, NLON), BF16),
            pltpu.VMEM((8, 128, 128), F32),
            pltpu.VMEM((W, 40, 128), BF16),
            pltpu.VMEM((W, 40, 128), BF16),
            pltpu.VMEM((4, 160, 128), F32),
            DMA((2,)),
            DMA,
            DMA,
        ],
        compiler_params=params(0),
        name="to_spectral",
    )(lat_order, gauss_weights, lat_row, pair_row, grid, table)
    solved = pl.pallas_call(
        kernel_b,
        out_shape=jax.ShapeDtypeStruct((8 * SLOTS, COLS), F32),
        in_specs=[SMEM, VMEM, VMEM, VMEM, VMEM, VMEM, HBM],
        out_specs=VMEM,
        scratch_shapes=[
            pltpu.VMEM((SLOTS, LAT, COLS), BF16),
            pltpu.VMEM((NB, ROWS, 128), BF16),
            pltpu.VMEM((LV, ROWS, 128), BF16),
            pltpu.VMEM((LV, ROWS, 128), BF16),
            pltpu.VMEM((NB, ROWS, 128), BF16),
            pltpu.VMEM((256, 128), F32),
            DMA((SLOTS,)),
            DMA((2,)),
            DMA((2,)),
        ],
        compiler_params=params(1),
        name="vertical",
    )(
        slot_pair,
        field_slots.reshape(1, 256),
        stiffness.reshape(1, 128),
        grouped,
        modes_in,
        modes_out,
        legendre,
    )
    product = pl.pallas_call(
        kernel_c,
        out_shape=jax.ShapeDtypeStruct((JL, ROWS, NLON), BF16),
        in_specs=[SMEM, VMEM, VMEM, VMEM, HBM, HBM, HBM],
        out_specs=VMEM,
        scratch_shapes=[
            pltpu.VMEM((SLOTS, LAT, COLS), BF16),
            pltpu.VMEM((JL, ROWS, NLON), BF16),
            pltpu.VMEM((640, NLON), BF16),
            pltpu.VMEM((8, 128, 128), F32),
            pltpu.VMEM((160, LAT), BF16),
            pltpu.VMEM((4, 160, 128), F32),
            pltpu.VMEM((W, 40, 128), BF16),
            pltpu.VMEM((W, 40, 128), BF16),
            pltpu.VMEM((640, 128), F32),
            DMA((SLOTS + 2,)),
            DMA,
            DMA,
        ],
        compiler_params=params(2),
        name="to_grid",
    )(slot_pair, lat_row, pair_row, solved, legendre, grid, table)
    return jnp.transpose(product, (1, 0, 2))


def solution(mesh):
    in_specs = (P("lev", "wave", None), P("wave", None, None), P(), P(), P(), P(), P(), P(), P())
    out_specs = P("lev", "wave", None)
    return jax.shard_map(local, mesh=mesh, in_specs=in_specs, out_specs=out_specs, check_vma=False)
```

```python
import functools

import jax
import jax.numpy as jnp
import numpy as np
from jax import lax
from jax.experimental import pallas as pl
from jax.experimental.pallas import tpu as pltpu
from jax.sharding import PartitionSpec as P

NM = 320
LEVELS = 128
W = 16
LV = 64
ROWS = 4
JL = 30
JP = 32
SLOTS = 10
LAT = 480
COLS = 384
NB = 60
NLON = 1024
F32 = jnp.float32
BF16 = jnp.bfloat16
MESH = pl.DeviceIdType.MESH
HBM = pl.BlockSpec(memory_space=pltpu.HBM)
VMEM = pltpu.VMEM
SMEM = pltpu.SMEM
DMA = pltpu.SemaphoreType.DMA


def fourier_rows():
    steps = (np.arange(NM)[:, None] * np.arange(NLON)[None, :]) % NLON
    angles = steps.astype(np.float32) * np.float32(2.0 * np.pi / NLON)
    entries = np.stack([np.cos(angles), -np.sin(angles)], axis=1) / np.float32(32.0)
    return entries.reshape(2 * NM, NLON).astype(jnp.bfloat16)


def iota(shape, axis):
    return lax.broadcasted_iota(jnp.int32, shape, axis)


def one_hot(condition):
    return jnp.where(condition, 1.0, 0.0).astype(F32).astype(BF16)


def dot(a, b):
    return jnp.dot(a, b, preferred_element_type=F32)


def dot_nt(a, b):
    return lax.dot_general(a, b, (((1,), (1,)), ((), ())), preferred_element_type=F32)


def far_first(step):
    half = (step + 1) // 2
    return 4 + jnp.where(step % 2 == 0, half, -half)


def wave_partner(step):
    w = lax.axis_index("wave")
    z = (w // 2 + far_first(step // 2)) % 8
    return z * 2 + (w % 2 + 1 - step % 2) % 2


def lev_partner(step):
    me = lax.axis_index("lev")
    x = (me // 8 + far_first(step // 8)) % 8
    y = (me % 8 + far_first(step % 8)) % 8
    return x * 8 + y


def each(count, body):
    def step(i, carry):
        body(i)
        return carry

    lax.fori_loop(0, count, step, 0, unroll=True)


def enter():
    barrier = pltpu.get_barrier_semaphore()

    def greet_lev(i):
        pl.semaphore_signal(
            barrier, inc=1, device_id={"lev": lev_partner(i)}, device_id_type=MESH
        )

    def greet_wave(i):
        pl.semaphore_signal(
            barrier, inc=1, device_id={"wave": wave_partner(i)}, device_id_type=MESH
        )

    each(LV - 1, greet_lev)
    each(W - 1, greet_wave)


def wait_bytes(ref, count, sem):
    part = ref.at[pl.ds(0, count)]
    pltpu.make_async_copy(part, part, sem).wait()


def lat_selector(lat):
    j = iota((LAT, W * JP), 0)
    jp = iota((LAT, W * JP), 1)
    local = jp & (JP - 1)
    spread = one_hot((j == (jp >> 5) * JL + local) & (local < JL))
    high = jnp.broadcast_to((lat >> 5).astype(F32), (8, LAT)).astype(BF16)
    low = jnp.broadcast_to((lat & 31).astype(F32), (8, LAT)).astype(BF16)
    there = dot(high, spread)[0:1] * 32.0 + dot(low, spread)[0:1]
    there = jnp.where((iota((1, W * JP), 1) & (JP - 1)) < JL, there, -1.0)
    return one_hot(iota((LAT, W * JP), 0).astype(F32) == there)


def table_rows(pair, index):
    wave = jnp.where((index & 2) == 0, pair, (NM - 1.0) - pair)
    return 2.0 * wave + (index & 1).astype(F32)


def to_slots(pair):
    pair = jnp.broadcast_to(pair.astype(F32), (128, 160)).astype(BF16)
    repeat = one_hot((iota((640, 160), 0) >> 2) == iota((640, 160), 1))
    target = table_rows(dot_nt(repeat, pair), iota((640, 128), 0))
    blocks = [
        one_hot(target == (iota((640, 128), 1) + 128 * b).astype(F32)) for b in range(5)
    ]
    return jnp.concatenate(blocks, axis=1)


def from_slots(pair):
    pair = jnp.broadcast_to(pair.astype(F32), (8, 160)).astype(BF16)
    repeat = one_hot(iota((160, 640), 0) == (iota((160, 640), 1) >> 2))
    target = table_rows(dot(pair, repeat)[0:1], iota((1, 640), 1))
    return one_hot(iota((640, 640), 0).astype(F32) == target)


def rows_to_lanes(pieces):
    return [
        jnp.concatenate([piece[:, JP * b : JP * b + JP] for piece in pieces], axis=1)
        for b in range(4)
    ]


def joined(ref):
    return jnp.concatenate([ref[b] for b in range(ref.shape[0])], axis=1)


def send_wave(send_buf, recv_buf, send_sem, recv_sem):
    w = lax.axis_index("wave")

    def send(i):
        to = wave_partner(i)
        pltpu.make_async_remote_copy(
            src_ref=send_buf.at[to],
            dst_ref=recv_buf.at[w],
            send_sem=send_sem,
            recv_sem=recv_sem,
            device_id={"wave": to},
            device_id_type=MESH,
        ).start()

    each(W - 1, send)
    recv_buf[w] = send_buf[w]


def send_lev(send_buf, recv_buf, send_sem, recv_sem, limit):
    me = lax.axis_index("lev")

    def send(i):
        to = lev_partner(i)

        def start():
            pltpu.make_async_remote_copy(
                src_ref=send_buf.at[to],
                dst_ref=recv_buf.at[me],
                send_sem=send_sem,
                recv_sem=recv_sem,
                device_id={"lev": to},
                device_id_type=MESH,
            ).start()

        if limit == LV:
            start()
        else:
            pl.when(to < limit)(start)

    each(LV - 1, send)


def kernel(
    lat_hbm, gauss_hbm, pair_hbm, lat_row, pair_row, slots_row, stiff_row, modes_in_hbm,
    modes_out_hbm, grid_hbm, table_hbm, basis_hbm, out_ref,
    lat_s, gauss_s, pair_s, lat_v, pair_v, slots_v, stiff_v, modes_in_v, modes_out_v, grid_v,
    table_v, basis, spread, send_a, recv_a, mixed, degrees, selector, slot_rows, modes_a,
    modes_b, factor_v, out_b, in_b, back_b, home_b, rows_f, send_c, recv_c, slotted,
    copy_sem, send_sem, recv_sem,
):
    w = lax.axis_index("wave")
    me = lax.axis_index("lev")
    works = me < NB
    enter()
    pairs = [
        (grid_hbm, grid_v), (pair_row, pair_v), (lat_hbm, lat_s), (gauss_hbm, gauss_s),
        (table_hbm, table_v), (pair_hbm, pair_s), (lat_row, lat_v), (slots_row, slots_v),
        (stiff_row, stiff_v), (modes_in_hbm, modes_in_v), (modes_out_hbm, modes_out_v),
        (basis_hbm, basis),
    ]
    gets = [pltpu.make_async_copy(a, b, copy_sem.at[i]) for i, (a, b) in enumerate(pairs)]
    for get in gets:
        get.start()

    gets[1].wait()
    slot_order = to_slots(pair_v[...])
    spread[...] = jnp.zeros_like(spread)
    gets[0].wait()
    for jl in range(JL):
        rows = grid_v[jl].astype(F32)
        for b in range(8):
            spread[b, pl.ds(jl, ROWS, stride=JP), :] = rows[:, 128 * b : 128 * b + 128]
    values = joined(spread).astype(BF16)
    gets[2].wait()
    gets[3].wait()
    lane = iota((1, 128), 1)

    def add_weight(jl, weight):
        value = gauss_s[lat_s[w * JL + jl]]
        return jnp.where((lane & (JP - 1)) == jl, value, weight)

    weight = lax.fori_loop(0, JL, add_weight, jnp.zeros((1, 128), F32), unroll=True)
    gets[4].wait()
    fourier = (dot_nt(table_v[...], values) * weight).astype(BF16)
    slots = dot(slot_order, fourier)
    for d in range(W):
        send_a[d] = slots[40 * d : 40 * d + 40].astype(BF16)
    pl.semaphore_wait(pltpu.get_barrier_semaphore(), LV + W - 2)
    send_wave(send_a, recv_a, send_sem.at[0], recv_sem.at[0])

    for get in gets[5:11]:
        get.wait()
    selector[...] = lat_selector(lat_v[...])
    picks = [
        one_hot((iota((LEVELS, 256), 0) + LEVELS * f) == slots_v[...]) for f in range(2)
    ]
    modes = jnp.concatenate([dot(modes_in_v[...], pick) for pick in picks], axis=0)
    modes_a[...] = modes.astype(BF16)
    modes_t = jnp.transpose(modes_out_v[...].astype(F32)).astype(BF16)
    modes = jnp.concatenate([dot(modes_t, pick) for pick in picks], axis=0)
    modes_b[...] = jnp.transpose(modes).astype(BF16)
    stiffness = jnp.transpose(jnp.broadcast_to(stiff_v[...], (128, 128)))
    own_pair = pair_s[w * SLOTS + lax.min(me, NB - 1) // 6]
    column = lane + (me % 3) * 128
    degree = jnp.where(column < NM - own_pair, own_pair + column, column - 1).astype(F32)
    growth = degree * (degree + 1.0) / (NM * NM)
    factor_v[...] = 1.0 / (1.0 + growth * stiffness)
    slot_rows[...] = from_slots(pair_v[...])
    gets[11].wait()

    wait_bytes(recv_a, W - 1, recv_sem.at[0])
    for g in range(4):
        pieces = rows_to_lanes([recv_a[4 * g + s].astype(F32) for s in range(4)])
        for r in range(ROWS):
            mixed[g, pl.ds(r, 40, stride=ROWS), :] = pieces[r]
    degrees[...] = dot_nt(joined(mixed).astype(BF16), selector[...]).astype(BF16)
    all_columns = iota((8, COLS), 1)
    firsts = [all_columns < NM - pair_s[w * SLOTS + k] for k in range(SLOTS)]
    for k in range(SLOTS):
        both = dot(degrees[16 * k : 16 * k + 16], basis[k])
        picked = jnp.where(firsts[k], both[0:8], both[8:16])
        for q in range(2):
            for c in range(3):
                out_b[6 * k + 3 * q + c] = picked[
                    4 * q : 4 * q + 4, 128 * c : 128 * c + 128
                ].astype(BF16)
    send_lev(out_b, in_b, send_sem.at[1], recv_sem.at[1], NB)

    @pl.when(works)
    def _():
        in_b[me] = out_b[me]
        wait_bytes(in_b, LV - 1, recv_sem.at[1])
        for s in range(LV):
            rows_f[4 * s : 4 * s + 4] = in_b[s].astype(F32)
        modal = dot(modes_a[...], rows_f[...].astype(BF16))
        factor = factor_v[...]
        modal = jnp.concatenate([modal[:128] * factor, modal[128:] * factor], axis=0)
        rows_f[...] = dot(modes_b[...], modal.astype(BF16))
        for s in range(LV):
            back_b[s] = rows_f[4 * s : 4 * s + 4].astype(BF16)
        send_lev(back_b, home_b, send_sem.at[2], recv_sem.at[2], LV)
        home_b[me] = back_b[me]
        wait_bytes(home_b, NB - 1, recv_sem.at[2])

    @pl.when(jnp.logical_not(works))
    def _():
        wait_bytes(home_b, NB, recv_sem.at[2])

    for k in range(SLOTS):
        values = jnp.concatenate(
            [
                jnp.concatenate(
                    [home_b[6 * k + 3 * q + c].astype(F32) for c in range(3)], axis=1
                )
                for q in range(2)
            ],
            axis=0,
        )
        both = jnp.concatenate(
            [jnp.where(firsts[k], values, 0.0), jnp.where(firsts[k], 0.0, values)], axis=0
        )
        degrees[16 * k : 16 * k + 16] = dot_nt(both.astype(BF16), basis[k]).astype(BF16)
    there = dot(degrees[...], selector[...])
    for g in range(4):
        mixed[g] = there[:, 128 * g : 128 * g + 128]
    for g in range(4):
        pieces = rows_to_lanes(
            [mixed[g, pl.ds(r, 40, stride=ROWS), :] for r in range(ROWS)]
        )
        for s in range(4):
            send_c[4 * g + s] = pieces[s].astype(BF16)
    send_wave(send_c, recv_c, send_sem.at[3], recv_sem.at[3])

    @pl.when(works)
    def _():
        wait_bytes(out_b, NB - 1, send_sem.at[1])
        wait_bytes(back_b, LV - 1, send_sem.at[2])

    @pl.when(jnp.logical_not(works))
    def _():
        wait_bytes(out_b, NB, send_sem.at[1])

    wait_bytes(send_a, W - 1, send_sem.at[0])

    wait_bytes(recv_c, W - 1, recv_sem.at[3])
    for d in range(W):
        slotted[40 * d : 40 * d + 40] = recv_c[d].astype(F32)
    natural = dot(slot_rows[...], slotted[...].astype(BF16))
    fields = dot(jnp.transpose(natural).astype(BF16), table_v[...])
    for b in range(8):
        spread[b] = spread[b] * fields[:, 128 * b : 128 * b + 128]
    for jl in range(JL):
        for b in range(8):
            rows = spread[b, pl.ds(jl, ROWS, stride=JP), :]
            out_ref[jl, :, 128 * b : 128 * b + 128] = rows.astype(BF16)
    wait_bytes(send_c, W - 1, send_sem.at[3])


def local(
    grid_values,
    legendre,
    gauss_weights,
    modes_in,
    modes_out,
    stiffness,
    slot_pair,
    lat_order,
    field_slots,
):
    product = pl.pallas_call(
        kernel,
        out_shape=jax.ShapeDtypeStruct((JL, ROWS, NLON), BF16),
        in_specs=[HBM] * 12,
        out_specs=pl.BlockSpec(memory_space=VMEM),
        scratch_shapes=[
            SMEM((LAT,), jnp.int32),
            SMEM((LAT,), F32),
            SMEM((160,), jnp.int32),
            VMEM((1, LAT), jnp.int32),
            VMEM((1, 160), jnp.int32),
            VMEM((1, 256), jnp.int32),
            VMEM((1, 128), F32),
            VMEM((LEVELS, LEVELS), BF16),
            VMEM((LEVELS, LEVELS), BF16),
            VMEM((JL, ROWS, NLON), BF16),
            VMEM((640, NLON), BF16),
            VMEM((SLOTS, LAT, COLS), BF16),
            VMEM((8, 128, 128), F32),
            VMEM((W, 40, 128), BF16),
            VMEM((W, 40, 128), BF16),
            VMEM((4, 160, 128), F32),
            VMEM((160, LAT), BF16),
            VMEM((LAT, W * JP), BF16),
            VMEM((640, 640), BF16),
            VMEM((256, 256), BF16),
            VMEM((256, 256), BF16),
            VMEM((LEVELS, 128), F32),
            VMEM((NB, ROWS, 128), BF16),
            VMEM((LV, ROWS, 128), BF16),
            VMEM((LV, ROWS, 128), BF16),
            VMEM((NB, ROWS, 128), BF16),
            VMEM((256, 128), F32),
            VMEM((W, 40, 128), BF16),
            VMEM((W, 40, 128), BF16),
            VMEM((640, 128), F32),
            DMA((12,)),
            DMA((4,)),
            DMA((4,)),
        ],
        compiler_params=pltpu.CompilerParams(
            collective_id=0, has_side_effects=True, vmem_limit_bytes=60 << 20
        ),
        name="transform_step",
    )(
        lat_order,
        gauss_weights,
        slot_pair,
        lat_order.reshape(1, LAT),
        slot_pair.reshape(1, 160),
        field_slots.reshape(1, 256),
        stiffness.reshape(1, 128),
        modes_in,
        modes_out,
        jnp.transpose(grid_values, (1, 0, 2)),
        jnp.asarray(fourier_rows()),
        legendre,
    )
    return jnp.transpose(product, (1, 0, 2))


def solution(mesh):
    in_specs = (P("lev", "wave", None), P("wave", None, None), P(), P(), P(), P(), P(), P(), P())
    out_specs = P("lev", "wave", None)
    return jax.shard_map(local, mesh=mesh, in_specs=in_specs, out_specs=out_specs, check_vma=False)
```

```python
import functools

import jax
import jax.numpy as jnp
import numpy as np
from jax import lax
from jax.experimental import pallas as pl
from jax.experimental.pallas import tpu as pltpu
from jax.sharding import PartitionSpec as P

NM = 320
LEVELS = 128
W = 16
LV = 64
ROWS = 4
JL = 30
JP = 32
SLOTS = 10
LAT = 480
COLS = 384
NB = 60
NLON = 1024
F32 = jnp.float32
BF16 = jnp.bfloat16
MESH = pl.DeviceIdType.MESH
HBM = pl.BlockSpec(memory_space=pltpu.HBM)
VMEM = pltpu.VMEM
SMEM = pltpu.SMEM
DMA = pltpu.SemaphoreType.DMA


def fourier_rows():
    steps = (np.arange(NM)[:, None] * np.arange(NLON)[None, :]) % NLON
    angles = steps.astype(np.float32) * np.float32(2.0 * np.pi / NLON)
    entries = np.stack([np.cos(angles), -np.sin(angles)], axis=1) / np.float32(32.0)
    return entries.reshape(2 * NM, NLON).astype(jnp.bfloat16)


def iota(shape, axis):
    return lax.broadcasted_iota(jnp.int32, shape, axis)


def one_hot(condition):
    return jnp.where(condition, 1.0, 0.0).astype(F32).astype(BF16)


def dot(a, b):
    return jnp.dot(a, b, preferred_element_type=F32)


def dot_nt(a, b):
    return lax.dot_general(a, b, (((1,), (1,)), ((), ())), preferred_element_type=F32)


def ring_distance(step):
    return min(step, 8 - step)


WAVE_STEPS = sorted(
    [(z, core) for z in range(8) for core in range(2) if z or core],
    key=lambda step: -ring_distance(step[0]),
)
LEV_STEPS = sorted(
    [(x, y) for x in range(8) for y in range(8) if x or y],
    key=lambda step: -ring_distance(step[0]) - ring_distance(step[1]),
)
RING_STEPS = sorted(range(1, 8), key=lambda step: -ring_distance(step))


def wave_partners():
    w = lax.axis_index("wave")
    z, core = lax.div(w, 2), lax.rem(w, 2)
    chips = [lax.rem(z + step, 8) * 2 for step in range(8)]
    cores = [core, 1 - core]
    return [chips[a] + cores[b] for a, b in WAVE_STEPS]


def lev_places():
    me = lax.axis_index("lev")
    x, y = lax.div(me, 8), lax.rem(me, 8)
    return (
        [lax.rem(x + step, 8) * 8 for step in range(8)],
        [lax.rem(y + step, 8) for step in range(8)],
    )


def lev_partners():
    xs, ys = lev_places()
    return [xs[a] + ys[b] for a, b in LEV_STEPS]


def signal(semaphore, axis, to):
    pl.semaphore_signal(semaphore, inc=1, device_id={axis: to}, device_id_type=MESH)


def enter():
    barrier = pltpu.get_barrier_semaphore()
    xs, ys = lev_places()
    for step in RING_STEPS:
        signal(barrier, "lev", xs[step] + ys[0])
        signal(barrier, "lev", xs[0] + ys[step])
    for to in wave_partners():
        signal(barrier, "wave", to)


def pass_on(semaphore):
    xs, ys = lev_places()
    for step in RING_STEPS:
        signal(semaphore, "lev", xs[0] + ys[step])


def wait_bytes(ref, count, sem):
    part = ref.at[pl.ds(0, count)]
    pltpu.make_async_copy(part, part, sem).wait()


def lat_selector(lat):
    j = iota((LAT, W * JP), 0)
    jp = iota((LAT, W * JP), 1)
    local = jp & (JP - 1)
    spread = one_hot((j == (jp >> 5) * JL + local) & (local < JL))
    high = jnp.broadcast_to((lat >> 5).astype(F32), (8, LAT)).astype(BF16)
    low = jnp.broadcast_to((lat & 31).astype(F32), (8, LAT)).astype(BF16)
    there = dot(high, spread)[0:1] * 32.0 + dot(low, spread)[0:1]
    there = jnp.where((iota((1, W * JP), 1) & (JP - 1)) < JL, there, -1.0)
    return one_hot(iota((LAT, W * JP), 0).astype(F32) == there)


def table_rows(pair, index):
    wave = jnp.where((index & 2) == 0, pair, (NM - 1.0) - pair)
    return 2.0 * wave + (index & 1).astype(F32)


def to_slots(pair):
    pair = jnp.broadcast_to(pair.astype(F32), (128, 160)).astype(BF16)
    repeat = one_hot((iota((640, 160), 0) >> 2) == iota((640, 160), 1))
    target = table_rows(dot_nt(repeat, pair), iota((640, 128), 0))
    blocks = [
        one_hot(target == (iota((640, 128), 1) + 128 * b).astype(F32)) for b in range(5)
    ]
    return jnp.concatenate(blocks, axis=1)


def rows_to_lanes(pieces):
    return [
        jnp.concatenate([piece[:, JP * b : JP * b + JP] for piece in pieces], axis=1)
        for b in range(4)
    ]


def joined(ref):
    return jnp.concatenate([ref[b] for b in range(ref.shape[0])], axis=1)


def send_wave(send_buf, recv_buf, send_sem, recv_sem):
    w = lax.axis_index("wave")
    for to in wave_partners():
        pltpu.make_async_remote_copy(
            src_ref=send_buf.at[to],
            dst_ref=recv_buf.at[w],
            send_sem=send_sem,
            recv_sem=recv_sem,
            device_id={"wave": to},
            device_id_type=MESH,
        ).start()
    recv_buf[w] = send_buf[w]


def send_lev(send_buf, recv_buf, send_sem, recv_sem, limit):
    me = lax.axis_index("lev")
    for to in lev_partners():
        copy = pltpu.make_async_remote_copy(
            src_ref=send_buf.at[to],
            dst_ref=recv_buf.at[me],
            send_sem=send_sem,
            recv_sem=recv_sem,
            device_id={"lev": to},
            device_id_type=MESH,
        )
        if limit == LV:
            copy.start()
        else:
            pl.when(to < limit)(copy.start)


def kernel(
    lat_hbm, gauss_hbm, pair_hbm, lat_row, pair_row, slots_row, stiff_row, modes_in_hbm,
    modes_out_hbm, grid_hbm, table_hbm, basis_hbm, out_ref,
    lat_s, gauss_s, pair_s, lat_v, pair_v, slots_v, stiff_v, modes_in_v, modes_out_v, grid_v,
    table_v, basis, spread, send_a, recv_a, mixed, degrees, selector, slot_order, slot_table, modes_a,
    modes_b, factor_v, out_b, in_b, back_b, home_b, rows_f, send_c, recv_c, slotted,
    copy_sem, send_sem, recv_sem, ring_sem,
):
    w = lax.axis_index("wave")
    me = lax.axis_index("lev")
    works = me < NB
    pairs = [
        (grid_hbm, grid_v), (pair_row, pair_v), (lat_hbm, lat_s), (gauss_hbm, gauss_s),
        (table_hbm, table_v), (pair_hbm, pair_s), (lat_row, lat_v), (slots_row, slots_v),
        (stiff_row, stiff_v), (modes_in_hbm, modes_in_v), (modes_out_hbm, modes_out_v),
        (basis_hbm, basis),
    ]
    gets = [pltpu.make_async_copy(a, b, copy_sem.at[i]) for i, (a, b) in enumerate(pairs)]
    for get in gets:
        get.start()
    enter()

    gets[1].wait()
    slot_order[...] = to_slots(pair_v[...])
    spread[...] = jnp.zeros_like(spread)
    gets[0].wait()
    for jl in range(JL):
        rows = grid_v[jl].astype(F32)
        for b in range(8):
            spread[b, pl.ds(jl, ROWS, stride=JP), :] = rows[:, 128 * b : 128 * b + 128]
    values = joined(spread).astype(BF16)
    gets[2].wait()
    gets[3].wait()
    lane = iota((1, 128), 1)

    def add_weight(jl, weight):
        value = gauss_s[lat_s[w * JL + jl]]
        return jnp.where((lane & (JP - 1)) == jl, value, weight)

    weight = lax.fori_loop(0, JL, add_weight, jnp.zeros((1, 128), F32), unroll=True)
    gets[4].wait()
    fourier = (dot_nt(table_v[...], values) * weight).astype(BF16)
    slots = dot(slot_order[...], fourier)
    for d in range(W):
        send_a[d] = slots[40 * d : 40 * d + 40].astype(BF16)
    pl.semaphore_wait(pltpu.get_barrier_semaphore(), W - 1 + 14)
    pass_on(ring_sem)
    send_wave(send_a, recv_a, send_sem.at[0], recv_sem.at[0])

    for get in gets[5:11]:
        get.wait()
    selector[...] = lat_selector(lat_v[...])
    picks = [
        one_hot((iota((LEVELS, 256), 0) + LEVELS * f) == slots_v[...]) for f in range(2)
    ]
    modes = jnp.concatenate([dot(modes_in_v[...], pick) for pick in picks], axis=0)
    modes_a[...] = modes.astype(BF16)
    modes_t = jnp.transpose(modes_out_v[...].astype(F32)).astype(BF16)
    modes = jnp.concatenate([dot(modes_t, pick) for pick in picks], axis=0)
    modes_b[...] = jnp.transpose(modes).astype(BF16)
    stiffness = jnp.transpose(jnp.broadcast_to(stiff_v[...], (128, 128)))
    own_pair = pair_s[w * SLOTS + lax.min(me, NB - 1) // 6]
    column = lane + (me % 3) * 128
    degree = jnp.where(column < NM - own_pair, own_pair + column, column - 1).astype(F32)
    growth = degree * (degree + 1.0) / (NM * NM)
    factor_v[...] = 1.0 / (1.0 + growth * stiffness)
    gets[11].wait()

    wait_bytes(recv_a, W - 1, recv_sem.at[0])
    for g in range(4):
        pieces = rows_to_lanes([recv_a[4 * g + s].astype(F32) for s in range(4)])
        for r in range(ROWS):
            mixed[g, pl.ds(r, 40, stride=ROWS), :] = pieces[r]
    degrees[...] = dot_nt(joined(mixed).astype(BF16), selector[...]).astype(BF16)
    all_columns = iota((8, COLS), 1)
    firsts = [all_columns < NM - pair_s[w * SLOTS + k] for k in range(SLOTS)]
    for k in range(SLOTS):
        both = dot(degrees[16 * k : 16 * k + 16], basis[k])
        picked = jnp.where(firsts[k], both[0:8], both[8:16])
        for q in range(2):
            for c in range(3):
                out_b[6 * k + 3 * q + c] = picked[
                    4 * q : 4 * q + 4, 128 * c : 128 * c + 128
                ].astype(BF16)
    pl.semaphore_wait(ring_sem, 7)
    send_lev(out_b, in_b, send_sem.at[1], recv_sem.at[1], NB)

    for b in range(5):
        part = pl.ds(128 * b, 128)
        slot_table[part] = dot(slot_order[part], table_v[...]).astype(BF16)

    @pl.when(works)
    def _():
        in_b[me] = out_b[me]
        wait_bytes(in_b, LV - 1, recv_sem.at[1])
        for s in range(LV):
            rows_f[4 * s : 4 * s + 4] = in_b[s].astype(F32)
        modal = dot(modes_a[...], rows_f[...].astype(BF16))
        factor = factor_v[...]
        modal = jnp.concatenate([modal[:128] * factor, modal[128:] * factor], axis=0)
        rows_f[...] = dot(modes_b[...], modal.astype(BF16))
        for s in range(LV):
            back_b[s] = rows_f[4 * s : 4 * s + 4].astype(BF16)
        send_lev(back_b, home_b, send_sem.at[2], recv_sem.at[2], LV)
        home_b[me] = back_b[me]
        wait_bytes(home_b, NB - 1, recv_sem.at[2])

    @pl.when(jnp.logical_not(works))
    def _():
        wait_bytes(home_b, NB, recv_sem.at[2])

    for k in range(SLOTS):
        values = jnp.concatenate(
            [
                jnp.concatenate(
                    [home_b[6 * k + 3 * q + c].astype(F32) for c in range(3)], axis=1
                )
                for q in range(2)
            ],
            axis=0,
        )
        both = jnp.concatenate(
            [jnp.where(firsts[k], values, 0.0), jnp.where(firsts[k], 0.0, values)], axis=0
        )
        degrees[16 * k : 16 * k + 16] = dot_nt(both.astype(BF16), basis[k]).astype(BF16)
    there = dot(degrees[...], selector[...])
    for g in range(4):
        mixed[g] = there[:, 128 * g : 128 * g + 128]
    for g in range(4):
        pieces = rows_to_lanes(
            [mixed[g, pl.ds(r, 40, stride=ROWS), :] for r in range(ROWS)]
        )
        for s in range(4):
            send_c[4 * g + s] = pieces[s].astype(BF16)
    send_wave(send_c, recv_c, send_sem.at[3], recv_sem.at[3])

    @pl.when(works)
    def _():
        wait_bytes(out_b, NB - 1, send_sem.at[1])
        wait_bytes(back_b, LV - 1, send_sem.at[2])

    @pl.when(jnp.logical_not(works))
    def _():
        wait_bytes(out_b, NB, send_sem.at[1])

    wait_bytes(send_a, W - 1, send_sem.at[0])

    wait_bytes(recv_c, W - 1, recv_sem.at[3])
    for d in range(W):
        slotted[40 * d : 40 * d + 40] = recv_c[d].astype(F32)
    fields = dot(jnp.transpose(slotted[...]).astype(BF16), slot_table[...])
    for b in range(8):
        spread[b] = spread[b] * fields[:, 128 * b : 128 * b + 128]
    for jl in range(JL):
        for b in range(8):
            rows = spread[b, pl.ds(jl, ROWS, stride=JP), :]
            out_ref[jl, :, 128 * b : 128 * b + 128] = rows.astype(BF16)
    wait_bytes(send_c, W - 1, send_sem.at[3])


def local(
    grid_values,
    legendre,
    gauss_weights,
    modes_in,
    modes_out,
    stiffness,
    slot_pair,
    lat_order,
    field_slots,
):
    product = pl.pallas_call(
        kernel,
        out_shape=VMEM((JL, ROWS, NLON), BF16),
        in_specs=[HBM] * 12,
        out_specs=pl.BlockSpec(memory_space=VMEM),
        scratch_shapes=[
            SMEM((LAT,), jnp.int32),
            SMEM((LAT,), F32),
            SMEM((160,), jnp.int32),
            VMEM((1, LAT), jnp.int32),
            VMEM((1, 160), jnp.int32),
            VMEM((1, 256), jnp.int32),
            VMEM((1, 128), F32),
            VMEM((LEVELS, LEVELS), BF16),
            VMEM((LEVELS, LEVELS), BF16),
            VMEM((JL, ROWS, NLON), BF16),
            VMEM((640, NLON), BF16),
            VMEM((SLOTS, LAT, COLS), BF16),
            VMEM((8, 128, 128), F32),
            VMEM((W, 40, 128), BF16),
            VMEM((W, 40, 128), BF16),
            VMEM((4, 160, 128), F32),
            VMEM((160, LAT), BF16),
            VMEM((LAT, W * JP), BF16),
            VMEM((640, 640), BF16),
            VMEM((640, NLON), BF16),
            VMEM((256, 256), BF16),
            VMEM((256, 256), BF16),
            VMEM((LEVELS, 128), F32),
            VMEM((NB, ROWS, 128), BF16),
            VMEM((LV, ROWS, 128), BF16),
            VMEM((LV, ROWS, 128), BF16),
            VMEM((NB, ROWS, 128), BF16),
            VMEM((256, 128), F32),
            VMEM((W, 40, 128), BF16),
            VMEM((W, 40, 128), BF16),
            VMEM((640, 128), F32),
            DMA((12,)),
            DMA((4,)),
            DMA((4,)),
            pltpu.SemaphoreType.REGULAR,
        ],
        compiler_params=pltpu.CompilerParams(
            collective_id=0, has_side_effects=True, vmem_limit_bytes=60 << 20
        ),
        name="transform_step",
    )(
        lat_order,
        gauss_weights,
        slot_pair,
        lat_order.reshape(1, LAT),
        slot_pair.reshape(1, 160),
        field_slots.reshape(1, 256),
        stiffness.reshape(1, 128),
        modes_in,
        modes_out,
        jnp.transpose(grid_values, (1, 0, 2)),
        jnp.asarray(fourier_rows()),
        legendre,
    )
    return jnp.transpose(product, (1, 0, 2))


def solution(mesh):
    in_specs = (P("lev", "wave", None), P("wave", None, None), P(), P(), P(), P(), P(), P(), P())
    out_specs = P("lev", "wave", None)
    return jax.shard_map(local, mesh=mesh, in_specs=in_specs, out_specs=out_specs, check_vma=False)
```

```python
import functools

import jax
import jax.numpy as jnp
import numpy as np
from jax import lax
from jax.experimental import pallas as pl
from jax.experimental.pallas import tpu as pltpu
from jax.sharding import PartitionSpec as P

NM = 320
LEVELS = 128
W = 16
LV = 64
ROWS = 4
JL = 30
JP = 32
SLOTS = 10
LAT = 480
COLS = 384
NB = 60
NLON = 1024
F32 = jnp.float32
BF16 = jnp.bfloat16
MESH = pl.DeviceIdType.MESH
HBM = pl.BlockSpec(memory_space=pltpu.HBM)
VMEM = pltpu.VMEM
SMEM = pltpu.SMEM
DMA = pltpu.SemaphoreType.DMA


def fourier_rows():
    steps = (np.arange(NM)[:, None] * np.arange(NLON)[None, :]) % NLON
    angles = steps.astype(np.float32) * np.float32(2.0 * np.pi / NLON)
    entries = np.stack([np.cos(angles), -np.sin(angles)], axis=1) / np.float32(32.0)
    return entries.reshape(2 * NM, NLON).astype(jnp.bfloat16)


def iota(shape, axis):
    return lax.broadcasted_iota(jnp.int32, shape, axis)


def one_hot(condition):
    return jnp.where(condition, 1.0, 0.0).astype(F32).astype(BF16)


def dot(a, b):
    return jnp.dot(a, b, preferred_element_type=F32)


def dot_nt(a, b):
    return lax.dot_general(a, b, (((1,), (1,)), ((), ())), preferred_element_type=F32)


def ring_distance(step):
    return min(step, 8 - step)


WAVE_STEPS = sorted(
    [(z, core) for z in range(8) for core in range(2) if z or core],
    key=lambda step: -ring_distance(step[0]),
)
LEV_STEPS = sorted(
    [(x, y) for x in range(8) for y in range(8) if x or y],
    key=lambda step: -ring_distance(step[0]) - ring_distance(step[1]),
)
RING_STEPS = sorted(range(1, 8), key=lambda step: -ring_distance(step))


def wave_partners():
    w = lax.axis_index("wave")
    z, core = lax.div(w, 2), lax.rem(w, 2)
    chips = [lax.rem(z + step, 8) * 2 for step in range(8)]
    cores = [core, 1 - core]
    return [chips[a] + cores[b] for a, b in WAVE_STEPS]


def lev_places():
    me = lax.axis_index("lev")
    x, y = lax.div(me, 8), lax.rem(me, 8)
    return (
        [lax.rem(x + step, 8) * 8 for step in range(8)],
        [lax.rem(y + step, 8) for step in range(8)],
    )


def lev_partners():
    xs, ys = lev_places()
    return [xs[a] + ys[b] for a, b in LEV_STEPS]


def signal(semaphore, axis, to):
    pl.semaphore_signal(semaphore, inc=1, device_id={axis: to}, device_id_type=MESH)


def enter():
    barrier = pltpu.get_barrier_semaphore()
    xs, ys = lev_places()
    for to in wave_partners():
        signal(barrier, "wave", to)
    for step in RING_STEPS:
        signal(barrier, "lev", xs[step] + ys[0])
        signal(barrier, "lev", xs[0] + ys[step])


def pass_on(semaphore):
    xs, ys = lev_places()
    for step in RING_STEPS:
        signal(semaphore, "lev", xs[0] + ys[step])


def wait_bytes(ref, count, sem):
    part = ref.at[pl.ds(0, count)]
    pltpu.make_async_copy(part, part, sem).wait()


def lat_selector(lat):
    j = iota((LAT, W * JP), 0)
    jp = iota((LAT, W * JP), 1)
    local = jp & (JP - 1)
    spread = one_hot((j == (jp >> 5) * JL + local) & (local < JL))
    high = jnp.broadcast_to((lat >> 5).astype(F32), (8, LAT)).astype(BF16)
    low = jnp.broadcast_to((lat & 31).astype(F32), (8, LAT)).astype(BF16)
    there = dot(high, spread)[0:1] * 32.0 + dot(low, spread)[0:1]
    there = jnp.where((iota((1, W * JP), 1) & (JP - 1)) < JL, there, -1.0)
    return one_hot(iota((LAT, W * JP), 0).astype(F32) == there)


def table_rows(pair, index):
    wave = jnp.where((index & 2) == 0, pair, (NM - 1.0) - pair)
    return 2.0 * wave + (index & 1).astype(F32)


def to_slots(pair):
    pair = jnp.broadcast_to(pair.astype(F32), (128, 160)).astype(BF16)
    repeat = one_hot((iota((640, 160), 0) >> 2) == iota((640, 160), 1))
    target = table_rows(dot_nt(repeat, pair), iota((640, 128), 0))
    blocks = [
        one_hot(target == (iota((640, 128), 1) + 128 * b).astype(F32)) for b in range(5)
    ]
    return jnp.concatenate(blocks, axis=1)


def rows_to_lanes(pieces):
    return [
        jnp.concatenate([piece[:, JP * b : JP * b + JP] for piece in pieces], axis=1)
        for b in range(4)
    ]


def joined(ref):
    return jnp.concatenate([ref[b] for b in range(ref.shape[0])], axis=1)


def send_wave(send_buf, recv_buf, send_sem, recv_sem):
    w = lax.axis_index("wave")
    for to in wave_partners():
        pltpu.make_async_remote_copy(
            src_ref=send_buf.at[to],
            dst_ref=recv_buf.at[w],
            send_sem=send_sem,
            recv_sem=recv_sem,
            device_id={"wave": to},
            device_id_type=MESH,
        ).start()
    recv_buf[w] = send_buf[w]


def lev_copy(send_buf, recv_buf, send_sem, recv_sem, to):
    return pltpu.make_async_remote_copy(
        src_ref=send_buf.at[to],
        dst_ref=recv_buf.at[lax.axis_index("lev")],
        send_sem=send_sem,
        recv_sem=recv_sem,
        device_id={"lev": to},
        device_id_type=MESH,
    )


def slots_by_distance():
    x = lax.div(lax.axis_index("lev"), 8)
    own = lax.min(lax.div(8 * x + 3, 6), SLOTS - 1)
    return [lax.rem(own + step, SLOTS) for step in (5, 4, 6, 3, 7, 2, 8, 1, 9, 0)]


def kernel(
    lat_hbm, gauss_hbm, pair_hbm, lat_row, pair_row, slots_row, stiff_row, modes_in_hbm,
    modes_out_hbm, grid_hbm, table_hbm, basis_hbm, out_ref,
    lat_s, gauss_s, pair_s, lat_v, pair_v, slots_v, stiff_v, modes_in_v, modes_out_v, grid_v,
    table_v, basis, spread, send_a, recv_a, mixed, degrees, selector, slot_order, slot_table, modes_a,
    modes_b, factor_v, out_b, in_b, back_b, home_b, rows_f, send_c, recv_c, slotted,
    copy_sem, send_sem, recv_sem, home_sem, ring_sem,
):
    w = lax.axis_index("wave")
    me = lax.axis_index("lev")
    works = me < NB
    pairs = [
        (grid_hbm, grid_v), (pair_row, pair_v), (lat_hbm, lat_s), (gauss_hbm, gauss_s),
        (table_hbm, table_v), (pair_hbm, pair_s), (lat_row, lat_v), (slots_row, slots_v),
        (stiff_row, stiff_v), (modes_in_hbm, modes_in_v), (modes_out_hbm, modes_out_v),
        (basis_hbm, basis),
    ]
    gets = [pltpu.make_async_copy(a, b, copy_sem.at[i]) for i, (a, b) in enumerate(pairs)]
    for get in gets:
        get.start()
    enter()

    gets[1].wait()
    slot_order[...] = to_slots(pair_v[...])
    spread[...] = jnp.zeros_like(spread)
    gets[0].wait()
    for jl in range(JL):
        rows = grid_v[jl].astype(F32)
        for b in range(8):
            spread[b, pl.ds(jl, ROWS, stride=JP), :] = rows[:, 128 * b : 128 * b + 128]
    values = joined(spread).astype(BF16)
    gets[2].wait()
    gets[3].wait()
    lane = iota((1, 128), 1)

    def add_weight(jl, weight):
        value = gauss_s[lat_s[w * JL + jl]]
        return jnp.where((lane & (JP - 1)) == jl, value, weight)

    weight = lax.fori_loop(0, JL, add_weight, jnp.zeros((1, 128), F32), unroll=True)
    gets[4].wait()
    fourier = (dot_nt(table_v[...], values) * weight).astype(BF16)
    slots = dot(slot_order[...], fourier)
    for d in range(W):
        send_a[d] = slots[40 * d : 40 * d + 40].astype(BF16)
    pl.semaphore_wait(pltpu.get_barrier_semaphore(), W - 1 + 14)
    pass_on(ring_sem)
    send_wave(send_a, recv_a, send_sem.at[0], recv_sem.at[0])

    for get in gets[5:11]:
        get.wait()
    selector[...] = lat_selector(lat_v[...])
    picks = [
        one_hot((iota((LEVELS, 256), 0) + LEVELS * f) == slots_v[...]) for f in range(2)
    ]
    modes = jnp.concatenate([dot(modes_in_v[...], pick) for pick in picks], axis=0)
    modes_a[...] = modes.astype(BF16)
    modes_t = jnp.transpose(modes_out_v[...].astype(F32)).astype(BF16)
    modes = jnp.concatenate([dot(modes_t, pick) for pick in picks], axis=0)
    modes_b[...] = jnp.transpose(modes).astype(BF16)
    stiffness = jnp.transpose(jnp.broadcast_to(stiff_v[...], (128, 128)))
    own_pair = pair_s[w * SLOTS + lax.min(me, NB - 1) // 6]
    column = lane + (me % 3) * 128
    degree = jnp.where(column < NM - own_pair, own_pair + column, column - 1).astype(F32)
    growth = degree * (degree + 1.0) / (NM * NM)
    factor_v[...] = 1.0 / (1.0 + growth * stiffness)
    gets[11].wait()

    wait_bytes(recv_a, W - 1, recv_sem.at[0])
    for g in range(4):
        pieces = rows_to_lanes([recv_a[4 * g + s].astype(F32) for s in range(4)])
        for r in range(ROWS):
            mixed[g, pl.ds(r, 40, stride=ROWS), :] = pieces[r]
    degrees[...] = dot_nt(joined(mixed).astype(BF16), selector[...]).astype(BF16)
    all_columns = iota((8, COLS), 1)
    order = slots_by_distance()

    def send_blocks(k):
        for j in range(6):
            copy = lev_copy(out_b, in_b, send_sem.at[1], recv_sem.at[1], 6 * k + j)
            pl.when(6 * k + j != me)(copy.start)

    pl.semaphore_wait(ring_sem, 7)
    before = None
    for k in order:
        both = dot(degrees[pl.ds(pl.multiple_of(16 * k, 16), 16)], basis[k])
        first = all_columns < NM - pair_s[w * SLOTS + k]
        picked = jnp.where(first, both[0:8], both[8:16])
        for q in range(2):
            for c in range(3):
                out_b[6 * k + (3 * q + c)] = picked[
                    4 * q : 4 * q + 4, 128 * c : 128 * c + 128
                ].astype(BF16)
        if before is not None:
            send_blocks(before)
        before = k
    send_blocks(before)

    for b in range(5):
        part = pl.ds(128 * b, 128)
        slot_table[part] = dot(slot_order[part], table_v[...]).astype(BF16)

    @pl.when(works)
    def _():
        in_b[me] = out_b[me]
        wait_bytes(in_b, LV - 1, recv_sem.at[1])
        for s in range(LV):
            rows_f[4 * s : 4 * s + 4] = in_b[s].astype(F32)
        modal = dot(modes_a[...], rows_f[...].astype(BF16))
        factor = factor_v[...]
        modal = jnp.concatenate([modal[:128] * factor, modal[128:] * factor], axis=0)
        rows_f[...] = dot(modes_b[...], modal.astype(BF16))
        for s in range(LV):
            back_b[s] = rows_f[4 * s : 4 * s + 4].astype(BF16)
        for to in lev_partners():
            lev_copy(back_b, home_b, send_sem.at[2], home_sem.at[lax.div(me, 6)], to).start()
        home_b[me] = back_b[me]

    for k in reversed(order):
        own = lax.div(me, 6) == k
        pl.when(own)(lambda k=k: wait_bytes(home_b, 5, home_sem.at[k]))
        pl.when(jnp.logical_not(own))(lambda k=k: wait_bytes(home_b, 6, home_sem.at[k]))
        values = jnp.concatenate(
            [
                jnp.concatenate(
                    [home_b[6 * k + (3 * q + c)].astype(F32) for c in range(3)], axis=1
                )
                for q in range(2)
            ],
            axis=0,
        )
        first = all_columns < NM - pair_s[w * SLOTS + k]
        both = jnp.concatenate(
            [jnp.where(first, values, 0.0), jnp.where(first, 0.0, values)], axis=0
        )
        back = dot_nt(both.astype(BF16), basis[k]).astype(BF16)
        degrees[pl.ds(pl.multiple_of(16 * k, 16), 16)] = back
    there = dot(degrees[...], selector[...])
    for g in range(4):
        mixed[g] = there[:, 128 * g : 128 * g + 128]
    for g in range(4):
        pieces = rows_to_lanes(
            [mixed[g, pl.ds(r, 40, stride=ROWS), :] for r in range(ROWS)]
        )
        for s in range(4):
            send_c[4 * g + s] = pieces[s].astype(BF16)
    send_wave(send_c, recv_c, send_sem.at[3], recv_sem.at[3])

    @pl.when(works)
    def _():
        wait_bytes(out_b, NB - 1, send_sem.at[1])
        wait_bytes(back_b, LV - 1, send_sem.at[2])

    @pl.when(jnp.logical_not(works))
    def _():
        wait_bytes(out_b, NB, send_sem.at[1])

    wait_bytes(send_a, W - 1, send_sem.at[0])

    wait_bytes(recv_c, W - 1, recv_sem.at[3])
    for d in range(W):
        slotted[40 * d : 40 * d + 40] = recv_c[d].astype(F32)
    fields = dot(jnp.transpose(slotted[...]).astype(BF16), slot_table[...])
    for b in range(8):
        spread[b] = spread[b] * fields[:, 128 * b : 128 * b + 128]
    for jl in range(JL):
        for b in range(8):
            rows = spread[b, pl.ds(jl, ROWS, stride=JP), :]
            out_ref[jl, :, 128 * b : 128 * b + 128] = rows.astype(BF16)
    wait_bytes(send_c, W - 1, send_sem.at[3])


def local(
    grid_values,
    legendre,
    gauss_weights,
    modes_in,
    modes_out,
    stiffness,
    slot_pair,
    lat_order,
    field_slots,
):
    product = pl.pallas_call(
        kernel,
        out_shape=VMEM((JL, ROWS, NLON), BF16),
        in_specs=[HBM] * 12,
        out_specs=pl.BlockSpec(memory_space=VMEM),
        scratch_shapes=[
            SMEM((LAT,), jnp.int32),
            SMEM((LAT,), F32),
            SMEM((160,), jnp.int32),
            VMEM((1, LAT), jnp.int32),
            VMEM((1, 160), jnp.int32),
            VMEM((1, 256), jnp.int32),
            VMEM((1, 128), F32),
            VMEM((LEVELS, LEVELS), BF16),
            VMEM((LEVELS, LEVELS), BF16),
            VMEM((JL, ROWS, NLON), BF16),
            VMEM((640, NLON), BF16),
            VMEM((SLOTS, LAT, COLS), BF16),
            VMEM((8, 128, 128), F32),
            VMEM((W, 40, 128), BF16),
            VMEM((W, 40, 128), BF16),
            VMEM((4, 160, 128), F32),
            VMEM((160, LAT), BF16),
            VMEM((LAT, W * JP), BF16),
            VMEM((640, 640), BF16),
            VMEM((640, NLON), BF16),
            VMEM((256, 256), BF16),
            VMEM((256, 256), BF16),
            VMEM((LEVELS, 128), F32),
            VMEM((NB, ROWS, 128), BF16),
            VMEM((LV, ROWS, 128), BF16),
            VMEM((LV, ROWS, 128), BF16),
            VMEM((NB, ROWS, 128), BF16),
            VMEM((256, 128), F32),
            VMEM((W, 40, 128), BF16),
            VMEM((W, 40, 128), BF16),
            VMEM((640, 128), F32),
            DMA((12,)),
            DMA((4,)),
            DMA((4,)),
            DMA((SLOTS,)),
            pltpu.SemaphoreType.REGULAR,
        ],
        compiler_params=pltpu.CompilerParams(
            collective_id=0, has_side_effects=True, vmem_limit_bytes=60 << 20
        ),
        name="transform_step",
    )(
        lat_order,
        gauss_weights,
        slot_pair,
        lat_order.reshape(1, LAT),
        slot_pair.reshape(1, 160),
        field_slots.reshape(1, 256),
        stiffness.reshape(1, 128),
        modes_in,
        modes_out,
        jnp.transpose(grid_values, (1, 0, 2)),
        jnp.asarray(fourier_rows()),
        legendre,
    )
    return jnp.transpose(product, (1, 0, 2))


def solution(mesh):
    in_specs = (P("lev", "wave", None), P("wave", None, None), P(), P(), P(), P(), P(), P(), P())
    out_specs = P("lev", "wave", None)
    return jax.shard_map(local, mesh=mesh, in_specs=in_specs, out_specs=out_specs, check_vma=False)
```

```python
import functools

import jax
import jax.numpy as jnp
import numpy as np
from jax import lax
from jax.experimental import pallas as pl
from jax.experimental.pallas import tpu as pltpu
from jax.sharding import PartitionSpec as P

NM = 320
LEVELS = 128
W = 16
LV = 64
ROWS = 4
JL = 30
JP = 32
SLOTS = 10
LAT = 480
COLS = 384
NB = 60
NLON = 1024
PARTS = ((0, 4), (4, SLOTS))
F32 = jnp.float32
BF16 = jnp.bfloat16
MESH = pl.DeviceIdType.MESH
HBM = pl.BlockSpec(memory_space=pltpu.HBM)
VMEM = pltpu.VMEM
SMEM = pltpu.SMEM
DMA = pltpu.SemaphoreType.DMA


def fourier_rows():
    steps = (np.arange(NM)[:, None] * np.arange(NLON)[None, :]) % NLON
    angles = steps.astype(np.float32) * np.float32(2.0 * np.pi / NLON)
    entries = np.stack([np.cos(angles), -np.sin(angles)], axis=1) / np.float32(32.0)
    return entries.reshape(2 * NM, NLON).astype(jnp.bfloat16)


def iota(shape, axis):
    return lax.broadcasted_iota(jnp.int32, shape, axis)


def one_hot(condition):
    return jnp.where(condition, 1.0, 0.0).astype(F32).astype(BF16)


def dot(a, b):
    return jnp.dot(a, b, preferred_element_type=F32)


def dot_nt(a, b):
    return lax.dot_general(a, b, (((1,), (1,)), ((), ())), preferred_element_type=F32)


def ring_distance(step):
    return min(step, 8 - step)


WAVE_STEPS = sorted(
    [(z, core) for z in range(8) for core in range(2) if z or core],
    key=lambda step: -ring_distance(step[0]),
)
LEV_STEPS = sorted(
    [(x, y) for x in range(8) for y in range(8) if x or y],
    key=lambda step: -ring_distance(step[0]) - ring_distance(step[1]),
)
RING_STEPS = sorted(range(1, 8), key=lambda step: -ring_distance(step))


def wave_partners():
    w = lax.axis_index("wave")
    z, core = lax.div(w, 2), lax.rem(w, 2)
    chips = [lax.rem(z + step, 8) * 2 for step in range(8)]
    cores = [core, 1 - core]
    return [chips[a] + cores[b] for a, b in WAVE_STEPS]


def lev_places():
    me = lax.axis_index("lev")
    x, y = lax.div(me, 8), lax.rem(me, 8)
    return (
        [lax.rem(x + step, 8) * 8 for step in range(8)],
        [lax.rem(y + step, 8) for step in range(8)],
    )


def lev_partners():
    xs, ys = lev_places()
    return [xs[a] + ys[b] for a, b in LEV_STEPS]


def signal(semaphore, axis, to):
    pl.semaphore_signal(semaphore, inc=1, device_id={axis: to}, device_id_type=MESH)


def enter():
    barrier = pltpu.get_barrier_semaphore()
    xs, ys = lev_places()
    for step in RING_STEPS:
        signal(barrier, "lev", xs[step] + ys[0])
        signal(barrier, "lev", xs[0] + ys[step])
    for to in wave_partners():
        signal(barrier, "wave", to)


def pass_on(semaphore):
    xs, ys = lev_places()
    for step in RING_STEPS:
        signal(semaphore, "lev", xs[0] + ys[step])


def wait_bytes(ref, count, sem):
    part = ref.at[pl.ds(0, count)]
    pltpu.make_async_copy(part, part, sem).wait()


def lat_selector(lat):
    j = iota((LAT, W * JP), 0)
    jp = iota((LAT, W * JP), 1)
    local = jp & (JP - 1)
    spread = one_hot((j == (jp >> 5) * JL + local) & (local < JL))
    high = jnp.broadcast_to((lat >> 5).astype(F32), (8, LAT)).astype(BF16)
    low = jnp.broadcast_to((lat & 31).astype(F32), (8, LAT)).astype(BF16)
    there = dot(high, spread)[0:1] * 32.0 + dot(low, spread)[0:1]
    there = jnp.where((iota((1, W * JP), 1) & (JP - 1)) < JL, there, -1.0)
    return one_hot(iota((LAT, W * JP), 0).astype(F32) == there)


def table_rows(pair, index):
    wave = jnp.where((index & 2) == 0, pair, (NM - 1.0) - pair)
    return 2.0 * wave + (index & 1).astype(F32)


def to_slots(pair):
    pair = jnp.broadcast_to(pair.astype(F32), (128, 160)).astype(BF16)
    repeat = one_hot((iota((640, 160), 0) >> 2) == iota((640, 160), 1))
    target = table_rows(dot_nt(repeat, pair), iota((640, 128), 0))
    blocks = [
        one_hot(target == (iota((640, 128), 1) + 128 * b).astype(F32)) for b in range(5)
    ]
    return jnp.concatenate(blocks, axis=1)


def rows_to_lanes(pieces):
    return [
        jnp.concatenate([piece[:, JP * b : JP * b + JP] for piece in pieces], axis=1)
        for b in range(4)
    ]


def joined(ref):
    return jnp.concatenate([ref[b] for b in range(ref.shape[0])], axis=1)


def send_wave(send_buf, recv_buf, send_sem, recv_sem):
    w = lax.axis_index("wave")
    for to in wave_partners():
        pltpu.make_async_remote_copy(
            src_ref=send_buf.at[to],
            dst_ref=recv_buf.at[w],
            send_sem=send_sem,
            recv_sem=recv_sem,
            device_id={"wave": to},
            device_id_type=MESH,
        ).start()
    recv_buf[w] = send_buf[w]


def send_lev(send_buf, recv_buf, send_sem, recv_sem, limit):
    me = lax.axis_index("lev")
    for to in lev_partners():
        copy = pltpu.make_async_remote_copy(
            src_ref=send_buf.at[to],
            dst_ref=recv_buf.at[me],
            send_sem=send_sem,
            recv_sem=recv_sem,
            device_id={"lev": to},
            device_id_type=MESH,
        )
        if limit == LV:
            copy.start()
        else:
            pl.when(to < limit)(copy.start)


def kernel(
    lat_hbm, gauss_hbm, pair_hbm, lat_row, pair_row, slots_row, stiff_row, modes_in_hbm,
    modes_out_hbm, grid_hbm, table_hbm, basis_hbm, out_ref,
    lat_s, gauss_s, pair_s, lat_v, pair_v, slots_v, stiff_v, modes_in_v, modes_out_v, grid_v,
    table_v, basis, spread, send_a0, send_a1, recv_a0, recv_a1, mixed, degrees, selector, slot_order,
    slot_table0, slot_table1, modes_a, modes_b, factor_v, out_b, in_b, back_b, home_b, rows_f,
    send_c0, send_c1, recv_c0, recv_c1, slotted, fields_v,
    copy_sem, send_sem, recv_sem, ring_sem,
):
    w = lax.axis_index("wave")
    me = lax.axis_index("lev")
    works = me < NB
    send_a, recv_a = (send_a0, send_a1), (recv_a0, recv_a1)
    send_c, recv_c = (send_c0, send_c1), (recv_c0, recv_c1)
    slot_table = (slot_table0, slot_table1)
    pairs = [
        (grid_hbm, grid_v), (pair_row, pair_v), (lat_hbm, lat_s), (gauss_hbm, gauss_s),
        (table_hbm, table_v), (pair_hbm, pair_s), (lat_row, lat_v), (slots_row, slots_v),
        (stiff_row, stiff_v), (modes_in_hbm, modes_in_v), (modes_out_hbm, modes_out_v),
        (basis_hbm, basis),
    ]
    gets = [pltpu.make_async_copy(a, b, copy_sem.at[i]) for i, (a, b) in enumerate(pairs)]
    for get in gets:
        get.start()
    enter()

    gets[1].wait()
    slot_order[...] = to_slots(pair_v[...])
    spread[...] = jnp.zeros_like(spread)
    gets[0].wait()
    for jl in range(JL):
        rows = grid_v[jl].astype(F32)
        for b in range(8):
            spread[b, pl.ds(jl, ROWS, stride=JP), :] = rows[:, 128 * b : 128 * b + 128]
    values = joined(spread).astype(BF16)
    gets[2].wait()
    gets[3].wait()
    lane = iota((1, 128), 1)

    def add_weight(jl, weight):
        value = gauss_s[lat_s[w * JL + jl]]
        return jnp.where((lane & (JP - 1)) == jl, value, weight)

    weight = lax.fori_loop(0, JL, add_weight, jnp.zeros((1, 128), F32), unroll=True)
    gets[4].wait()
    fourier = (dot_nt(table_v[...], values) * weight).astype(BF16)
    slots = dot(slot_order[...], fourier)
    for d in range(W):
        for part, (start, end) in enumerate(PARTS):
            send_a[part][d] = slots[40 * d + 4 * start : 40 * d + 4 * end].astype(BF16)
    pl.semaphore_wait(pltpu.get_barrier_semaphore(), W - 1 + 14)
    pass_on(ring_sem)
    for part in range(2):
        send_wave(send_a[part], recv_a[part], send_sem.at[part], recv_sem.at[part])

    for get in gets[5:11]:
        get.wait()
    selector[...] = lat_selector(lat_v[...])
    picks = [
        one_hot((iota((LEVELS, 256), 0) + LEVELS * f) == slots_v[...]) for f in range(2)
    ]
    modes = jnp.concatenate([dot(modes_in_v[...], pick) for pick in picks], axis=0)
    modes_a[...] = modes.astype(BF16)
    modes_t = jnp.transpose(modes_out_v[...].astype(F32)).astype(BF16)
    modes = jnp.concatenate([dot(modes_t, pick) for pick in picks], axis=0)
    modes_b[...] = jnp.transpose(modes).astype(BF16)
    stiffness = jnp.transpose(jnp.broadcast_to(stiff_v[...], (128, 128)))
    own_pair = pair_s[w * SLOTS + lax.min(me, NB - 1) // 6]
    column = lane + (me % 3) * 128
    degree = jnp.where(column < NM - own_pair, own_pair + column, column - 1).astype(F32)
    growth = degree * (degree + 1.0) / (NM * NM)
    factor_v[...] = 1.0 / (1.0 + growth * stiffness)
    gets[11].wait()

    all_columns = iota((8, COLS), 1)
    firsts = [all_columns < NM - pair_s[w * SLOTS + k] for k in range(SLOTS)]
    for part, (start, end) in enumerate(PARTS):
        wait_bytes(recv_a[part], W - 1, recv_sem.at[part])
        count = 4 * (end - start)
        rows = slice(16 * start, 16 * end)
        for g in range(4):
            pieces = rows_to_lanes(
                [recv_a[part][4 * g + s].astype(F32) for s in range(4)]
            )
            for r in range(ROWS):
                mixed[g, pl.ds(16 * start + r, count, stride=ROWS), :] = pieces[r]
        values = jnp.concatenate([mixed[g, rows] for g in range(4)], axis=1)
        degrees[rows] = dot_nt(values.astype(BF16), selector[...]).astype(BF16)
        for k in range(start, end):
            both = dot(degrees[16 * k : 16 * k + 16], basis[k])
            picked = jnp.where(firsts[k], both[0:8], both[8:16])
            for q in range(2):
                for c in range(3):
                    out_b[6 * k + 3 * q + c] = picked[
                        4 * q : 4 * q + 4, 128 * c : 128 * c + 128
                    ].astype(BF16)
    pl.semaphore_wait(ring_sem, 7)
    send_lev(out_b, in_b, send_sem.at[2], recv_sem.at[2], NB)

    for pair in range(W // 2):
        rows = dot(slot_order[80 * pair : 80 * pair + 80], table_v[...])
        for part, (start, end) in enumerate(PARTS):
            count = 8 * (end - start)
            picked = [rows[40 * d + 4 * start : 40 * d + 4 * end] for d in range(2)]
            picked = jnp.concatenate(picked, axis=0).astype(BF16)
            slot_table[part][count * pair : count * pair + count] = picked

    @pl.when(works)
    def _():
        in_b[me] = out_b[me]
        wait_bytes(in_b, LV - 1, recv_sem.at[2])
        for s in range(LV):
            rows_f[4 * s : 4 * s + 4] = in_b[s].astype(F32)
        modal = dot(modes_a[...], rows_f[...].astype(BF16))
        factor = factor_v[...]
        modal = jnp.concatenate([modal[:128] * factor, modal[128:] * factor], axis=0)
        rows_f[...] = dot(modes_b[...], modal.astype(BF16))
        for s in range(LV):
            back_b[s] = rows_f[4 * s : 4 * s + 4].astype(BF16)
        send_lev(back_b, home_b, send_sem.at[3], recv_sem.at[3], LV)
        home_b[me] = back_b[me]
        wait_bytes(home_b, NB - 1, recv_sem.at[3])

    @pl.when(jnp.logical_not(works))
    def _():
        wait_bytes(home_b, NB, recv_sem.at[3])

    for part, (start, end) in enumerate(PARTS):
        for k in range(start, end):
            values = jnp.concatenate(
                [
                    jnp.concatenate(
                        [home_b[6 * k + 3 * q + c].astype(F32) for c in range(3)], axis=1
                    )
                    for q in range(2)
                ],
                axis=0,
            )
            both = jnp.concatenate(
                [jnp.where(firsts[k], values, 0.0), jnp.where(firsts[k], 0.0, values)], axis=0
            )
            degrees[16 * k : 16 * k + 16] = dot_nt(both.astype(BF16), basis[k]).astype(BF16)
        rows = slice(16 * start, 16 * end)
        there = dot(degrees[rows], selector[...])
        for g in range(4):
            mixed[g, rows] = there[:, 128 * g : 128 * g + 128]
        count = 4 * (end - start)
        for g in range(4):
            pieces = rows_to_lanes(
                [mixed[g, pl.ds(16 * start + r, count, stride=ROWS), :] for r in range(ROWS)]
            )
            for s in range(4):
                send_c[part][4 * g + s] = pieces[s].astype(BF16)
        send_wave(send_c[part], recv_c[part], send_sem.at[4 + part], recv_sem.at[4 + part])

    @pl.when(works)
    def _():
        wait_bytes(out_b, NB - 1, send_sem.at[2])
        wait_bytes(back_b, LV - 1, send_sem.at[3])

    @pl.when(jnp.logical_not(works))
    def _():
        wait_bytes(out_b, NB, send_sem.at[2])

    for part in range(2):
        wait_bytes(send_a[part], W - 1, send_sem.at[part])

    for part, (start, end) in enumerate(PARTS):
        wait_bytes(recv_c[part], W - 1, recv_sem.at[4 + part])
        count = 4 * (end - start)
        for d in range(W):
            slotted[count * d : count * d + count] = recv_c[part][d].astype(F32)
        values = jnp.transpose(slotted[: W * count]).astype(BF16)
        fields = dot(values, slot_table[part][...])
        if part == 0:
            fields_v[...] = fields
    fields = fields_v[...] + fields
    for b in range(8):
        spread[b] = spread[b] * fields[:, 128 * b : 128 * b + 128]
    for jl in range(JL):
        for b in range(8):
            rows = spread[b, pl.ds(jl, ROWS, stride=JP), :]
            out_ref[jl, :, 128 * b : 128 * b + 128] = rows.astype(BF16)
    for part in range(2):
        wait_bytes(send_c[part], W - 1, send_sem.at[4 + part])


def local(
    grid_values,
    legendre,
    gauss_weights,
    modes_in,
    modes_out,
    stiffness,
    slot_pair,
    lat_order,
    field_slots,
):
    product = pl.pallas_call(
        kernel,
        out_shape=VMEM((JL, ROWS, NLON), BF16),
        in_specs=[HBM] * 12,
        out_specs=pl.BlockSpec(memory_space=VMEM),
        scratch_shapes=[
            SMEM((LAT,), jnp.int32),
            SMEM((LAT,), F32),
            SMEM((160,), jnp.int32),
            VMEM((1, LAT), jnp.int32),
            VMEM((1, 160), jnp.int32),
            VMEM((1, 256), jnp.int32),
            VMEM((1, 128), F32),
            VMEM((LEVELS, LEVELS), BF16),
            VMEM((LEVELS, LEVELS), BF16),
            VMEM((JL, ROWS, NLON), BF16),
            VMEM((640, NLON), BF16),
            VMEM((SLOTS, LAT, COLS), BF16),
            VMEM((8, 128, 128), F32),
            VMEM((W, 16, 128), BF16),
            VMEM((W, 24, 128), BF16),
            VMEM((W, 16, 128), BF16),
            VMEM((W, 24, 128), BF16),
            VMEM((4, 160, 128), F32),
            VMEM((160, LAT), BF16),
            VMEM((LAT, W * JP), BF16),
            VMEM((640, 640), BF16),
            VMEM((256, NLON), BF16),
            VMEM((384, NLON), BF16),
            VMEM((256, 256), BF16),
            VMEM((256, 256), BF16),
            VMEM((LEVELS, 128), F32),
            VMEM((NB, ROWS, 128), BF16),
            VMEM((LV, ROWS, 128), BF16),
            VMEM((LV, ROWS, 128), BF16),
            VMEM((NB, ROWS, 128), BF16),
            VMEM((256, 128), F32),
            VMEM((W, 16, 128), BF16),
            VMEM((W, 24, 128), BF16),
            VMEM((W, 16, 128), BF16),
            VMEM((W, 24, 128), BF16),
            VMEM((384, 128), F32),
            VMEM((128, NLON), F32),
            DMA((12,)),
            DMA((6,)),
            DMA((6,)),
            pltpu.SemaphoreType.REGULAR,
        ],
        compiler_params=pltpu.CompilerParams(
            collective_id=0, has_side_effects=True, vmem_limit_bytes=60 << 20
        ),
        name="transform_step",
    )(
        lat_order,
        gauss_weights,
        slot_pair,
        lat_order.reshape(1, LAT),
        slot_pair.reshape(1, 160),
        field_slots.reshape(1, 256),
        stiffness.reshape(1, 128),
        modes_in,
        modes_out,
        jnp.transpose(grid_values, (1, 0, 2)),
        jnp.asarray(fourier_rows()),
        legendre,
    )
    return jnp.transpose(product, (1, 0, 2))


def solution(mesh):
    in_specs = (P("lev", "wave", None), P("wave", None, None), P(), P(), P(), P(), P(), P(), P())
    out_specs = P("lev", "wave", None)
    return jax.shard_map(local, mesh=mesh, in_specs=in_specs, out_specs=out_specs, check_vma=False)
```

```python
import functools

import jax
import jax.numpy as jnp
import numpy as np
from jax import lax
from jax.experimental import pallas as pl
from jax.experimental.pallas import tpu as pltpu
from jax.sharding import PartitionSpec as P

NM = 320
LEVELS = 128
W = 16
LV = 64
ROWS = 4
JL = 30
JP = 32
SLOTS = 10
LAT = 480
COLS = 384
NB = 60
NLON = 1024
F32 = jnp.float32
BF16 = jnp.bfloat16
MESH = pl.DeviceIdType.MESH
HBM = pl.BlockSpec(memory_space=pltpu.HBM)
VMEM = pltpu.VMEM
SMEM = pltpu.SMEM
DMA = pltpu.SemaphoreType.DMA


def fourier_rows():
    steps = (np.arange(NM)[:, None] * np.arange(NLON)[None, :]) % NLON
    angles = steps.astype(np.float32) * np.float32(2.0 * np.pi / NLON)
    entries = np.stack([np.cos(angles), -np.sin(angles)], axis=1) / np.float32(32.0)
    return entries.reshape(2 * NM, NLON).astype(jnp.bfloat16)


def iota(shape, axis):
    return lax.broadcasted_iota(jnp.int32, shape, axis)


def one_hot(condition):
    return jnp.where(condition, 1.0, 0.0).astype(F32).astype(BF16)


def dot(a, b):
    return jnp.dot(a, b, preferred_element_type=F32)


def dot_nt(a, b):
    return lax.dot_general(a, b, (((1,), (1,)), ((), ())), preferred_element_type=F32)


def ring_distance(step):
    return min(step, 8 - step)


WAVE_STEPS = sorted(
    [(z, core) for z in range(8) for core in range(2) if z or core],
    key=lambda step: -ring_distance(step[0]),
)
LEV_STEPS = sorted(
    [(x, y) for x in range(8) for y in range(8) if x or y],
    key=lambda step: -ring_distance(step[0]) - ring_distance(step[1]),
)
RING_STEPS = sorted(range(1, 8), key=lambda step: -ring_distance(step))


def wave_partners():
    w = lax.axis_index("wave")
    z, core = lax.div(w, 2), lax.rem(w, 2)
    chips = [lax.rem(z + step, 8) * 2 for step in range(8)]
    cores = [core, 1 - core]
    return [chips[a] + cores[b] for a, b in WAVE_STEPS]


def lev_places():
    me = lax.axis_index("lev")
    x, y = lax.div(me, 8), lax.rem(me, 8)
    return (
        [lax.rem(x + step, 8) * 8 for step in range(8)],
        [lax.rem(y + step, 8) for step in range(8)],
    )


def lev_partners():
    xs, ys = lev_places()
    return [xs[a] + ys[b] for a, b in LEV_STEPS]


def signal(semaphore, axis, to):
    pl.semaphore_signal(semaphore, inc=1, device_id={axis: to}, device_id_type=MESH)


def enter():
    barrier = pltpu.get_barrier_semaphore()
    xs, ys = lev_places()
    for to in wave_partners():
        signal(barrier, "wave", to)
    for step in RING_STEPS:
        signal(barrier, "lev", xs[step] + ys[0])
        signal(barrier, "lev", xs[0] + ys[step])


def pass_on(semaphore):
    xs, ys = lev_places()
    for step in RING_STEPS:
        signal(semaphore, "lev", xs[0] + ys[step])


def wait_bytes(ref, count, sem):
    part = ref.at[pl.ds(0, count)]
    pltpu.make_async_copy(part, part, sem).wait()


def lat_selector(lat):
    j = iota((LAT, W * JP), 0)
    jp = iota((LAT, W * JP), 1)
    local = jp & (JP - 1)
    spread = one_hot((j == (jp >> 5) * JL + local) & (local < JL))
    high = jnp.broadcast_to((lat >> 5).astype(F32), (8, LAT)).astype(BF16)
    low = jnp.broadcast_to((lat & 31).astype(F32), (8, LAT)).astype(BF16)
    there = dot(high, spread)[0:1] * 32.0 + dot(low, spread)[0:1]
    there = jnp.where((iota((1, W * JP), 1) & (JP - 1)) < JL, there, -1.0)
    return one_hot(iota((LAT, W * JP), 0).astype(F32) == there)


def table_rows(pair, index):
    wave = jnp.where((index & 2) == 0, pair, (NM - 1.0) - pair)
    return 2.0 * wave + (index & 1).astype(F32)


def to_slots(pair):
    pair = jnp.broadcast_to(pair.astype(F32), (128, 160)).astype(BF16)
    repeat = one_hot((iota((640, 160), 0) >> 2) == iota((640, 160), 1))
    target = table_rows(dot_nt(repeat, pair), iota((640, 128), 0))
    blocks = [
        one_hot(target == (iota((640, 128), 1) + 128 * b).astype(F32)) for b in range(5)
    ]
    return jnp.concatenate(blocks, axis=1)


def rows_to_lanes(pieces):
    return [
        jnp.concatenate([piece[:, JP * b : JP * b + JP] for piece in pieces], axis=1)
        for b in range(4)
    ]


def joined(ref):
    return jnp.concatenate([ref[b] for b in range(ref.shape[0])], axis=1)


def send_wave(send_buf, recv_buf, send_sem, recv_sem):
    w = lax.axis_index("wave")
    for to in wave_partners():
        pltpu.make_async_remote_copy(
            src_ref=send_buf.at[to],
            dst_ref=recv_buf.at[w],
            send_sem=send_sem,
            recv_sem=recv_sem,
            device_id={"wave": to},
            device_id_type=MESH,
        ).start()
    recv_buf[w] = send_buf[w]


def send_lev(send_buf, recv_buf, send_sem, recv_sem, limit):
    me = lax.axis_index("lev")
    for to in lev_partners():
        copy = pltpu.make_async_remote_copy(
            src_ref=send_buf.at[to],
            dst_ref=recv_buf.at[me],
            send_sem=send_sem,
            recv_sem=recv_sem,
            device_id={"lev": to},
            device_id_type=MESH,
        )
        if limit == LV:
            copy.start()
        else:
            pl.when(to < limit)(copy.start)


def kernel(
    lat_hbm, gauss_hbm, pair_hbm, lat_row, pair_row, slots_row, stiff_row, modes_in_hbm,
    modes_out_hbm, grid_hbm, table_hbm, basis_hbm, out_ref,
    lat_s, gauss_s, pair_s, lat_v, pair_v, slots_v, stiff_v, modes_in_v, modes_out_v, grid_v,
    table_v, basis, spread, send_a, recv_a, mixed, degrees, selector, slot_order, slot_table, modes_a,
    modes_b, factor_v, out_b, in_b, back_b, home_b, rows_f, send_c, recv_c, slotted, grid_f,
    copy_sem, send_sem, recv_sem, ring_sem,
):
    w = lax.axis_index("wave")
    me = lax.axis_index("lev")
    works = me < NB
    pairs = [
        (grid_hbm, grid_v), (pair_row, pair_v), (lat_hbm, lat_s), (gauss_hbm, gauss_s),
        (table_hbm, table_v), (pair_hbm, pair_s), (lat_row, lat_v), (slots_row, slots_v),
        (stiff_row, stiff_v), (modes_in_hbm, modes_in_v), (modes_out_hbm, modes_out_v),
        (basis_hbm, basis),
    ]
    gets = [pltpu.make_async_copy(a, b, copy_sem.at[i]) for i, (a, b) in enumerate(pairs)]
    for get in gets:
        get.start()
    enter()

    gets[1].wait()
    slot_order[...] = to_slots(pair_v[...])
    spread[...] = jnp.zeros_like(spread)
    gets[0].wait()
    for jl in range(JL):
        rows = grid_v[jl].astype(F32)
        for b in range(8):
            spread[b, pl.ds(jl, ROWS, stride=JP), :] = rows[:, 128 * b : 128 * b + 128]
    values = joined(spread).astype(BF16)
    gets[2].wait()
    gets[3].wait()
    lane = iota((1, 128), 1)

    def add_weight(jl, weight):
        value = gauss_s[lat_s[w * JL + jl]]
        return jnp.where((lane & (JP - 1)) == jl, value, weight)

    weight = lax.fori_loop(0, JL, add_weight, jnp.zeros((1, 128), F32), unroll=True)
    gets[4].wait()
    fourier = (dot_nt(table_v[...], values) * weight).astype(BF16)
    slots = dot(slot_order[...], fourier)
    for d in range(W):
        send_a[d] = slots[40 * d : 40 * d + 40].astype(BF16)
    pl.semaphore_wait(pltpu.get_barrier_semaphore(), W - 1 + 14)
    pass_on(ring_sem)
    send_wave(send_a, recv_a, send_sem.at[0], recv_sem.at[0])

    for get in gets[5:11]:
        get.wait()
    selector[...] = lat_selector(lat_v[...])
    picks = [
        one_hot((iota((LEVELS, 256), 0) + LEVELS * f) == slots_v[...]) for f in range(2)
    ]
    modes = jnp.concatenate([dot(modes_in_v[...], pick) for pick in picks], axis=0)
    modes_a[...] = modes.astype(BF16)
    modes_t = jnp.transpose(modes_out_v[...].astype(F32)).astype(BF16)
    modes = jnp.concatenate([dot(modes_t, pick) for pick in picks], axis=0)
    modes_b[...] = jnp.transpose(modes).astype(BF16)
    stiffness = jnp.transpose(jnp.broadcast_to(stiff_v[...], (128, 128)))
    own_pair = pair_s[w * SLOTS + lax.min(me, NB - 1) // 6]
    column = lane + (me % 3) * 128
    degree = jnp.where(column < NM - own_pair, own_pair + column, column - 1).astype(F32)
    growth = degree * (degree + 1.0) / (NM * NM)
    factor_v[...] = 1.0 / (1.0 + growth * stiffness)
    gets[11].wait()

    wait_bytes(recv_a, W - 1, recv_sem.at[0])
    for g in range(4):
        pieces = rows_to_lanes([recv_a[4 * g + s].astype(F32) for s in range(4)])
        for r in range(ROWS):
            mixed[g, pl.ds(r, 40, stride=ROWS), :] = pieces[r]
    degrees[...] = dot_nt(joined(mixed).astype(BF16), selector[...]).astype(BF16)
    all_columns = iota((8, COLS), 1)
    firsts = [all_columns < NM - pair_s[w * SLOTS + k] for k in range(SLOTS)]
    for k in range(SLOTS):
        both = dot(degrees[16 * k : 16 * k + 16], basis[k])
        picked = jnp.where(firsts[k], both[0:8], both[8:16])
        for q in range(2):
            for c in range(3):
                out_b[6 * k + 3 * q + c] = picked[
                    4 * q : 4 * q + 4, 128 * c : 128 * c + 128
                ].astype(BF16)
    pl.semaphore_wait(ring_sem, 7)
    send_lev(out_b, in_b, send_sem.at[1], recv_sem.at[1], NB)

    for b in range(5):
        part = pl.ds(128 * b, 128)
        slot_table[part] = dot(slot_order[part], table_v[...]).astype(BF16)

    for jl in range(JL):
        grid_f[4 * jl : 4 * jl + 4] = grid_v[jl].astype(F32)

    @pl.when(works)
    def _():
        in_b[me] = out_b[me]
        wait_bytes(in_b, LV - 1, recv_sem.at[1])
        for s in range(LV):
            rows_f[4 * s : 4 * s + 4] = in_b[s].astype(F32)
        modal = dot(modes_a[...], rows_f[...].astype(BF16))
        factor = factor_v[...]
        modal = jnp.concatenate([modal[:128] * factor, modal[128:] * factor], axis=0)
        rows_f[...] = dot(modes_b[...], modal.astype(BF16))
        for s in range(LV):
            back_b[s] = rows_f[4 * s : 4 * s + 4].astype(BF16)
        send_lev(back_b, home_b, send_sem.at[2], recv_sem.at[2], LV)
        home_b[me] = back_b[me]
        wait_bytes(home_b, NB - 1, recv_sem.at[2])

    @pl.when(jnp.logical_not(works))
    def _():
        wait_bytes(home_b, NB, recv_sem.at[2])

    for k in range(SLOTS):
        values = jnp.concatenate(
            [
                jnp.concatenate(
                    [home_b[6 * k + 3 * q + c].astype(F32) for c in range(3)], axis=1
                )
                for q in range(2)
            ],
            axis=0,
        )
        both = jnp.concatenate(
            [jnp.where(firsts[k], values, 0.0), jnp.where(firsts[k], 0.0, values)], axis=0
        )
        degrees[16 * k : 16 * k + 16] = dot_nt(both.astype(BF16), basis[k]).astype(BF16)
    there = dot(degrees[...], selector[...])
    for g in range(4):
        mixed[g] = there[:, 128 * g : 128 * g + 128]
    for g in range(4):
        pieces = rows_to_lanes(
            [mixed[g, pl.ds(r, 40, stride=ROWS), :] for r in range(ROWS)]
        )
        for s in range(4):
            send_c[4 * g + s] = pieces[s].astype(BF16)
    send_wave(send_c, recv_c, send_sem.at[3], recv_sem.at[3])

    @pl.when(works)
    def _():
        wait_bytes(out_b, NB - 1, send_sem.at[1])
        wait_bytes(back_b, LV - 1, send_sem.at[2])

    @pl.when(jnp.logical_not(works))
    def _():
        wait_bytes(out_b, NB, send_sem.at[1])

    wait_bytes(send_a, W - 1, send_sem.at[0])

    wait_bytes(recv_c, W - 1, recv_sem.at[3])
    for d in range(W):
        slotted[40 * d : 40 * d + 40] = recv_c[d].astype(F32)
    point = iota((JL * ROWS, 128), 0)
    lanes = (point & 3) * JP + (point >> 2)
    to_points = one_hot(iota((JL * ROWS, 128), 1) == lanes)
    by_point = dot_nt(to_points, slotted[...].astype(BF16)).astype(BF16)
    products = dot(by_point, slot_table[...]) * grid_f[...]
    for jl in range(JL):
        out_ref[jl] = products[4 * jl : 4 * jl + 4].astype(BF16)
    wait_bytes(send_c, W - 1, send_sem.at[3])


def local(
    grid_values,
    legendre,
    gauss_weights,
    modes_in,
    modes_out,
    stiffness,
    slot_pair,
    lat_order,
    field_slots,
):
    product = pl.pallas_call(
        kernel,
        out_shape=VMEM((JL, ROWS, NLON), BF16),
        in_specs=[HBM] * 12,
        out_specs=pl.BlockSpec(memory_space=VMEM),
        scratch_shapes=[
            SMEM((LAT,), jnp.int32),
            SMEM((LAT,), F32),
            SMEM((160,), jnp.int32),
            VMEM((1, LAT), jnp.int32),
            VMEM((1, 160), jnp.int32),
            VMEM((1, 256), jnp.int32),
            VMEM((1, 128), F32),
            VMEM((LEVELS, LEVELS), BF16),
            VMEM((LEVELS, LEVELS), BF16),
            VMEM((JL, ROWS, NLON), BF16),
            VMEM((640, NLON), BF16),
            VMEM((SLOTS, LAT, COLS), BF16),
            VMEM((8, 128, 128), F32),
            VMEM((W, 40, 128), BF16),
            VMEM((W, 40, 128), BF16),
            VMEM((4, 160, 128), F32),
            VMEM((160, LAT), BF16),
            VMEM((LAT, W * JP), BF16),
            VMEM((640, 640), BF16),
            VMEM((640, NLON), BF16),
            VMEM((256, 256), BF16),
            VMEM((256, 256), BF16),
            VMEM((LEVELS, 128), F32),
            VMEM((NB, ROWS, 128), BF16),
            VMEM((LV, ROWS, 128), BF16),
            VMEM((LV, ROWS, 128), BF16),
            VMEM((NB, ROWS, 128), BF16),
            VMEM((256, 128), F32),
            VMEM((W, 40, 128), BF16),
            VMEM((W, 40, 128), BF16),
            VMEM((640, 128), F32),
            VMEM((JL * ROWS, NLON), F32),
            DMA((12,)),
            DMA((4,)),
            DMA((4,)),
            pltpu.SemaphoreType.REGULAR,
        ],
        compiler_params=pltpu.CompilerParams(
            collective_id=0, has_side_effects=True, vmem_limit_bytes=60 << 20
        ),
        name="transform_step",
    )(
        lat_order,
        gauss_weights,
        slot_pair,
        lat_order.reshape(1, LAT),
        slot_pair.reshape(1, 160),
        field_slots.reshape(1, 256),
        stiffness.reshape(1, 128),
        modes_in,
        modes_out,
        jnp.transpose(grid_values, (1, 0, 2)),
        jnp.asarray(fourier_rows()),
        legendre,
    )
    return jnp.transpose(product, (1, 0, 2))


def solution(mesh):
    in_specs = (P("lev", "wave", None), P("wave", None, None), P(), P(), P(), P(), P(), P(), P())
    out_specs = P("lev", "wave", None)
    return jax.shard_map(local, mesh=mesh, in_specs=in_specs, out_specs=out_specs, check_vma=False)
```

```python
import functools

import jax
import jax.numpy as jnp
import numpy as np
from jax import lax
from jax.experimental import pallas as pl
from jax.experimental.pallas import tpu as pltpu
from jax.sharding import PartitionSpec as P

NM = 320
LEVELS = 128
W = 16
LV = 64
ROWS = 4
JL = 30
JP = 32
SLOTS = 10
LAT = 480
COLS = 384
NB = 60
NLON = 1024
PARTS = ((0, 4), (4, SLOTS))
F32 = jnp.float32
BF16 = jnp.bfloat16
MESH = pl.DeviceIdType.MESH
HBM = pl.BlockSpec(memory_space=pltpu.HBM)
VMEM = pltpu.VMEM
SMEM = pltpu.SMEM
DMA = pltpu.SemaphoreType.DMA


def fourier_rows():
    steps = (np.arange(NM)[:, None] * np.arange(NLON)[None, :]) % NLON
    angles = steps.astype(np.float32) * np.float32(2.0 * np.pi / NLON)
    entries = np.stack([np.cos(angles), -np.sin(angles)], axis=1) / np.float32(32.0)
    return entries.reshape(2 * NM, NLON).astype(jnp.bfloat16)


def iota(shape, axis):
    return lax.broadcasted_iota(jnp.int32, shape, axis)


def one_hot(condition):
    return jnp.where(condition, 1.0, 0.0).astype(F32).astype(BF16)


def dot(a, b):
    return jnp.dot(a, b, preferred_element_type=F32)


def dot_nt(a, b):
    return lax.dot_general(a, b, (((1,), (1,)), ((), ())), preferred_element_type=F32)


def ring_distance(step):
    return min(step, 8 - step)


WAVE_STEPS = sorted(
    [(z, core) for z in range(8) for core in range(2) if z or core],
    key=lambda step: -ring_distance(step[0]),
)
LEV_STEPS = sorted(
    [(x, y) for x in range(8) for y in range(8) if x or y],
    key=lambda step: -ring_distance(step[0]) - ring_distance(step[1]),
)
RING_STEPS = sorted(range(1, 8), key=lambda step: -ring_distance(step))


def wave_partners():
    w = lax.axis_index("wave")
    z, core = lax.div(w, 2), lax.rem(w, 2)
    chips = [lax.rem(z + step, 8) * 2 for step in range(8)]
    cores = [core, 1 - core]
    return [chips[a] + cores[b] for a, b in WAVE_STEPS]


def lev_places():
    me = lax.axis_index("lev")
    x, y = lax.div(me, 8), lax.rem(me, 8)
    return (
        [lax.rem(x + step, 8) * 8 for step in range(8)],
        [lax.rem(y + step, 8) for step in range(8)],
    )


def lev_partners():
    xs, ys = lev_places()
    return [xs[a] + ys[b] for a, b in LEV_STEPS]


def signal(semaphore, axis, to):
    pl.semaphore_signal(semaphore, inc=1, device_id={axis: to}, device_id_type=MESH)


def enter():
    barrier = pltpu.get_barrier_semaphore()
    xs, ys = lev_places()
    for to in wave_partners():
        signal(barrier, "wave", to)
    for step in RING_STEPS:
        signal(barrier, "lev", xs[step] + ys[0])
        signal(barrier, "lev", xs[0] + ys[step])


def pass_on(semaphore):
    xs, ys = lev_places()
    for step in RING_STEPS:
        signal(semaphore, "lev", xs[0] + ys[step])


def wait_bytes(ref, count, sem):
    part = ref.at[pl.ds(0, count)]
    pltpu.make_async_copy(part, part, sem).wait()


def lat_selector(lat):
    j = iota((LAT, W * JP), 0)
    jp = iota((LAT, W * JP), 1)
    local = jp & (JP - 1)
    spread = one_hot((j == (jp >> 5) * JL + local) & (local < JL))
    high = jnp.broadcast_to((lat >> 5).astype(F32), (8, LAT)).astype(BF16)
    low = jnp.broadcast_to((lat & 31).astype(F32), (8, LAT)).astype(BF16)
    there = dot(high, spread)[0:1] * 32.0 + dot(low, spread)[0:1]
    there = jnp.where((iota((1, W * JP), 1) & (JP - 1)) < JL, there, -1.0)
    return one_hot(iota((LAT, W * JP), 0).astype(F32) == there)


def table_rows(pair, index):
    wave = jnp.where((index & 2) == 0, pair, (NM - 1.0) - pair)
    return 2.0 * wave + (index & 1).astype(F32)


def to_slots(pair):
    pair = jnp.broadcast_to(pair.astype(F32), (128, 160)).astype(BF16)
    repeat = one_hot((iota((640, 160), 0) >> 2) == iota((640, 160), 1))
    target = table_rows(dot_nt(repeat, pair), iota((640, 128), 0))
    blocks = [
        one_hot(target == (iota((640, 128), 1) + 128 * b).astype(F32)) for b in range(5)
    ]
    return jnp.concatenate(blocks, axis=1)


def rows_to_lanes(pieces):
    return [
        jnp.concatenate([piece[:, JP * b : JP * b + JP] for piece in pieces], axis=1)
        for b in range(4)
    ]


def joined(ref):
    return jnp.concatenate([ref[b] for b in range(ref.shape[0])], axis=1)


def send_wave(send_buf, recv_buf, send_sem, recv_sem):
    w = lax.axis_index("wave")
    for to in wave_partners():
        pltpu.make_async_remote_copy(
            src_ref=send_buf.at[to],
            dst_ref=recv_buf.at[w],
            send_sem=send_sem,
            recv_sem=recv_sem,
            device_id={"wave": to},
            device_id_type=MESH,
        ).start()
    recv_buf[w] = send_buf[w]


def lev_copy(send_buf, recv_buf, send_sem, recv_sem, to):
    return pltpu.make_async_remote_copy(
        src_ref=send_buf.at[to],
        dst_ref=recv_buf.at[lax.axis_index("lev")],
        send_sem=send_sem,
        recv_sem=recv_sem,
        device_id={"lev": to},
        device_id_type=MESH,
    )


def kernel(
    lat_hbm, gauss_hbm, pair_hbm, lat_row, pair_row, slots_row, stiff_row, modes_in_hbm,
    modes_out_hbm, grid_hbm, table_hbm, basis_hbm, out_ref,
    lat_s, gauss_s, pair_s, lat_v, pair_v, slots_v, stiff_v, modes_in_v, modes_out_v, grid_v,
    table_v, basis, spread, send_a0, send_a1, recv_a0, recv_a1, mixed, degrees, selector, slot_order, slot_table, modes_a,
    modes_b, factor_v, out_b, in_b, back_b, home_b, rows_f, send_c, recv_c, slotted, grid_f,
    copy_sem, send_sem, recv_sem, ring_sem,
):
    w = lax.axis_index("wave")
    me = lax.axis_index("lev")
    works = me < NB
    send_a, recv_a = (send_a0, send_a1), (recv_a0, recv_a1)
    pairs = [
        (grid_hbm, grid_v), (pair_row, pair_v), (lat_hbm, lat_s), (gauss_hbm, gauss_s),
        (table_hbm, table_v), (pair_hbm, pair_s), (lat_row, lat_v), (slots_row, slots_v),
        (stiff_row, stiff_v), (modes_in_hbm, modes_in_v), (modes_out_hbm, modes_out_v),
        (basis_hbm, basis),
    ]
    gets = [pltpu.make_async_copy(a, b, copy_sem.at[i]) for i, (a, b) in enumerate(pairs)]
    for get in gets:
        get.start()
    enter()

    gets[1].wait()
    slot_order[...] = to_slots(pair_v[...])
    spread[...] = jnp.zeros_like(spread)
    gets[0].wait()
    for jl in range(JL):
        rows = grid_v[jl].astype(F32)
        for b in range(8):
            spread[b, pl.ds(jl, ROWS, stride=JP), :] = rows[:, 128 * b : 128 * b + 128]
    values = joined(spread).astype(BF16)
    gets[2].wait()
    gets[3].wait()
    lane = iota((1, 128), 1)

    def add_weight(jl, weight):
        value = gauss_s[lat_s[w * JL + jl]]
        return jnp.where((lane & (JP - 1)) == jl, value, weight)

    weight = lax.fori_loop(0, JL, add_weight, jnp.zeros((1, 128), F32), unroll=True)
    gets[4].wait()
    fourier = (dot_nt(table_v[...], values) * weight).astype(BF16)
    slots = dot(slot_order[...], fourier)
    for d in range(W):
        for part, (start, end) in enumerate(PARTS):
            send_a[part][d] = slots[40 * d + 4 * start : 40 * d + 4 * end].astype(BF16)
    pl.semaphore_wait(pltpu.get_barrier_semaphore(), W - 1 + 14)
    pass_on(ring_sem)
    for part in range(2):
        send_wave(send_a[part], recv_a[part], send_sem.at[4 * part], recv_sem.at[4 * part])

    for get in gets[5:11]:
        get.wait()
    selector[...] = lat_selector(lat_v[...])
    picks = [
        one_hot((iota((LEVELS, 256), 0) + LEVELS * f) == slots_v[...]) for f in range(2)
    ]
    modes = jnp.concatenate([dot(modes_in_v[...], pick) for pick in picks], axis=0)
    modes_a[...] = modes.astype(BF16)
    modes_t = jnp.transpose(modes_out_v[...].astype(F32)).astype(BF16)
    modes = jnp.concatenate([dot(modes_t, pick) for pick in picks], axis=0)
    modes_b[...] = jnp.transpose(modes).astype(BF16)
    stiffness = jnp.transpose(jnp.broadcast_to(stiff_v[...], (128, 128)))
    own_pair = pair_s[w * SLOTS + lax.min(me, NB - 1) // 6]
    column = lane + (me % 3) * 128
    degree = jnp.where(column < NM - own_pair, own_pair + column, column - 1).astype(F32)
    growth = degree * (degree + 1.0) / (NM * NM)
    factor_v[...] = 1.0 / (1.0 + growth * stiffness)
    gets[11].wait()

    all_columns = iota((8, COLS), 1)
    firsts = [all_columns < NM - pair_s[w * SLOTS + k] for k in range(SLOTS)]
    for part, (start, end) in enumerate(PARTS):
        wait_bytes(recv_a[part], W - 1, recv_sem.at[4 * part])
        count = 4 * (end - start)
        rows = slice(16 * start, 16 * end)
        for g in range(4):
            pieces = rows_to_lanes(
                [recv_a[part][4 * g + s].astype(F32) for s in range(4)]
            )
            for r in range(ROWS):
                mixed[g, pl.ds(16 * start + r, count, stride=ROWS), :] = pieces[r]
        values = jnp.concatenate([mixed[g, rows] for g in range(4)], axis=1)
        degrees[rows] = dot_nt(values.astype(BF16), selector[...]).astype(BF16)
        for k in range(start, end):
            both = dot(degrees[16 * k : 16 * k + 16], basis[k])
            picked = jnp.where(firsts[k], both[0:8], both[8:16])
            for q in range(2):
                for c in range(3):
                    out_b[6 * k + 3 * q + c] = picked[
                        4 * q : 4 * q + 4, 128 * c : 128 * c + 128
                    ].astype(BF16)
        if part == 0:
            pl.semaphore_wait(ring_sem, 7)
            for to in range(6 * end):
                copy = lev_copy(out_b, in_b, send_sem.at[1], recv_sem.at[1], to)
                pl.when(to != me)(copy.start)
        else:
            for to in lev_partners():
                copy = lev_copy(out_b, in_b, send_sem.at[1], recv_sem.at[1], to)
                pl.when(jnp.logical_and(to >= 6 * start, to < NB))(copy.start)

    for b in range(5):
        part = pl.ds(128 * b, 128)
        slot_table[part] = dot(slot_order[part], table_v[...]).astype(BF16)

    for jl in range(JL):
        grid_f[4 * jl : 4 * jl + 4] = grid_v[jl].astype(F32)

    @pl.when(works)
    def _():
        in_b[me] = out_b[me]
        wait_bytes(in_b, LV - 1, recv_sem.at[1])
        for s in range(LV):
            rows_f[4 * s : 4 * s + 4] = in_b[s].astype(F32)
        modal = dot(modes_a[...], rows_f[...].astype(BF16))
        factor = factor_v[...]
        modal = jnp.concatenate([modal[:128] * factor, modal[128:] * factor], axis=0)
        rows_f[...] = dot(modes_b[...], modal.astype(BF16))
        for s in range(LV):
            back_b[s] = rows_f[4 * s : 4 * s + 4].astype(BF16)
        for to in lev_partners():
            lev_copy(back_b, home_b, send_sem.at[2], recv_sem.at[2], to).start()
        home_b[me] = back_b[me]
        wait_bytes(home_b, NB - 1, recv_sem.at[2])

    @pl.when(jnp.logical_not(works))
    def _():
        wait_bytes(home_b, NB, recv_sem.at[2])

    for k in range(SLOTS):
        values = jnp.concatenate(
            [
                jnp.concatenate(
                    [home_b[6 * k + 3 * q + c].astype(F32) for c in range(3)], axis=1
                )
                for q in range(2)
            ],
            axis=0,
        )
        both = jnp.concatenate(
            [jnp.where(firsts[k], values, 0.0), jnp.where(firsts[k], 0.0, values)], axis=0
        )
        degrees[16 * k : 16 * k + 16] = dot_nt(both.astype(BF16), basis[k]).astype(BF16)
    there = dot(degrees[...], selector[...])
    for g in range(4):
        mixed[g] = there[:, 128 * g : 128 * g + 128]
    for g in range(4):
        pieces = rows_to_lanes(
            [mixed[g, pl.ds(r, 40, stride=ROWS), :] for r in range(ROWS)]
        )
        for s in range(4):
            send_c[4 * g + s] = pieces[s].astype(BF16)
    send_wave(send_c, recv_c, send_sem.at[3], recv_sem.at[3])

    @pl.when(works)
    def _():
        wait_bytes(out_b, NB - 1, send_sem.at[1])
        wait_bytes(back_b, LV - 1, send_sem.at[2])

    @pl.when(jnp.logical_not(works))
    def _():
        wait_bytes(out_b, NB, send_sem.at[1])

    for part in range(2):
        wait_bytes(send_a[part], W - 1, send_sem.at[4 * part])

    wait_bytes(recv_c, W - 1, recv_sem.at[3])
    for d in range(W):
        slotted[40 * d : 40 * d + 40] = recv_c[d].astype(F32)
    point = iota((JL * ROWS, 128), 0)
    lanes = (point & 3) * JP + (point >> 2)
    to_points = one_hot(iota((JL * ROWS, 128), 1) == lanes)
    by_point = dot_nt(to_points, slotted[...].astype(BF16)).astype(BF16)
    products = dot(by_point, slot_table[...]) * grid_f[...]
    for jl in range(JL):
        out_ref[jl] = products[4 * jl : 4 * jl + 4].astype(BF16)
    wait_bytes(send_c, W - 1, send_sem.at[3])


def local(
    grid_values,
    legendre,
    gauss_weights,
    modes_in,
    modes_out,
    stiffness,
    slot_pair,
    lat_order,
    field_slots,
):
    product = pl.pallas_call(
        kernel,
        out_shape=VMEM((JL, ROWS, NLON), BF16),
        in_specs=[HBM] * 12,
        out_specs=pl.BlockSpec(memory_space=VMEM),
        scratch_shapes=[
            SMEM((LAT,), jnp.int32),
            SMEM((LAT,), F32),
            SMEM((160,), jnp.int32),
            VMEM((1, LAT), jnp.int32),
            VMEM((1, 160), jnp.int32),
            VMEM((1, 256), jnp.int32),
            VMEM((1, 128), F32),
            VMEM((LEVELS, LEVELS), BF16),
            VMEM((LEVELS, LEVELS), BF16),
            VMEM((JL, ROWS, NLON), BF16),
            VMEM((640, NLON), BF16),
            VMEM((SLOTS, LAT, COLS), BF16),
            VMEM((8, 128, 128), F32),
            VMEM((W, 16, 128), BF16),
            VMEM((W, 24, 128), BF16),
            VMEM((W, 16, 128), BF16),
            VMEM((W, 24, 128), BF16),
            VMEM((4, 160, 128), F32),
            VMEM((160, LAT), BF16),
            VMEM((LAT, W * JP), BF16),
            VMEM((640, 640), BF16),
            VMEM((640, NLON), BF16),
            VMEM((256, 256), BF16),
            VMEM((256, 256), BF16),
            VMEM((LEVELS, 128), F32),
            VMEM((NB, ROWS, 128), BF16),
            VMEM((LV, ROWS, 128), BF16),
            VMEM((LV, ROWS, 128), BF16),
            VMEM((NB, ROWS, 128), BF16),
            VMEM((256, 128), F32),
            VMEM((W, 40, 128), BF16),
            VMEM((W, 40, 128), BF16),
            VMEM((640, 128), F32),
            VMEM((JL * ROWS, NLON), F32),
            DMA((12,)),
            DMA((5,)),
            DMA((5,)),
            pltpu.SemaphoreType.REGULAR,
        ],
        compiler_params=pltpu.CompilerParams(
            collective_id=0, has_side_effects=True, vmem_limit_bytes=60 << 20
        ),
        name="transform_step",
    )(
        lat_order,
        gauss_weights,
        slot_pair,
        lat_order.reshape(1, LAT),
        slot_pair.reshape(1, 160),
        field_slots.reshape(1, 256),
        stiffness.reshape(1, 128),
        modes_in,
        modes_out,
        jnp.transpose(grid_values, (1, 0, 2)),
        jnp.asarray(fourier_rows()),
        legendre,
    )
    return jnp.transpose(product, (1, 0, 2))


def solution(mesh):
    in_specs = (P("lev", "wave", None), P("wave", None, None), P(), P(), P(), P(), P(), P(), P())
    out_specs = P("lev", "wave", None)
    return jax.shard_map(local, mesh=mesh, in_specs=in_specs, out_specs=out_specs, check_vma=False)
```
